32 devices in a mesh: groups: 2 (over x), frames: 16 (over z, y, core).
Axes of the slice: x: 2, y: 2, z: 4, core: 2. Of those that a mesh axis runs over, the one named last changes fastest.
Arguments:
- features: bfloat16 [4096, 1024], P(('groups', 'frames')), parts along dimension 0, may hold values from -6 to 6
- valid_length: int32 [2], P('groups'), parts along dimension 0, may hold values from 1024 to 2048
- ln1_gain: float32 [1024], replicated, may hold values from 0.5 to 1.5
- w_qkv: bfloat16 [1024, 1536], P('frames'), may hold values from -3 to 3
- w_out: bfloat16 [512, 1024], P('frames'), may hold values from -0.25 to 0.25
- ln2_gain: float32 [1024], replicated, may hold values from 0.5 to 1.5
- w_pw1: bfloat16 [1024, 2048], P('frames'), may hold values from -0.1875 to 0.1875
- w_dw: float32 [9, 1024], replicated, may hold values from -2 to 2
- bn_scale: float32 [1024], replicated, may hold values from 0.5 to 2
- bn_shift: float32 [1024], replicated, may hold values from -3 to 3
- w_pw2: bfloat16 [1024, 1024], P('frames'), may hold values from -0.1875 to 0.1875
Outputs:
- block_out: bfloat16 [4096, 1024], P(('groups', 'frames')), parts along dimension 0
The draws below stay inside these ranges and needn't reach their ends.
There are 2 independent parts, one for each index of `groups`. The reference program is written for one: setup_inputs(seed, part) draws one part's arguments, and reference() takes and returns one part's arrays. A program takes and returns all parts, laid end to end along the dimension named above; an argument that names none is the same for every part. Nothing has to cross between parts.
All inputs are finite; a program needn't handle non-finite values.
Results may differ from the reference program's by a relative error of at most 0.0098.
Values may be sent and summed in bfloat16 or wider, within the bound.
No kernel may reach another device: no remote copies, remote signals or barrier semaphores. Data moves between devices by JAX's collectives and lax.ppermute only.
A program may use at most 128 MiB of HBM per device.

```python
import math
import jax
import jax.numpy as jnp
from jax import lax

D = 1024
HEADS = 4
HD = 128
KERNEL = 9
FRAMES = 2048
ATT = 512
HALF = 4


def draw_w_qkv(key, part):
    first, second, third = jax.random.split(key, 3)
    root = 1.0 / math.sqrt(D)
    w_query = jax.random.normal(first, (D, ATT), jnp.float32) * (1.5 * root)
    w_key = jax.random.normal(second, (D, ATT), jnp.float32) * (1.5 * root)
    w_value = jax.random.normal(third, (D, ATT), jnp.float32) * root
    joined = jnp.concatenate([w_query, w_key, w_value], axis=1)
    return jnp.clip(joined, -3.0, 3.0).astype(jnp.bfloat16)


def block_scale(stream_key, dims, cuts, smallest, high):
    level = 1.0
    for axis_at, blocks in cuts:
        steps = jax.random.uniform(jax.random.fold_in(jax.random.fold_in(stream_key, 6), axis_at), (blocks,), jnp.float32, smallest / len(cuts), high / len(cuts))
        level = level * jnp.repeat(jnp.exp(steps), dims[axis_at] // blocks).reshape((-1,) + (1,) * (len(dims) - 1 - axis_at))
    return level


def gaussian(own_key, extent, deviation, most, pieces=(), held_as=jnp.bfloat16):
    factor_of = block_scale(own_key, extent, pieces, -0.22, 0.18) if pieces else 1.0
    array = jax.random.normal(own_key, extent, jnp.float32) * deviation * factor_of
    return jnp.minimum(jnp.maximum(array, -most), most).astype(held_as)


def setup_inputs(seed: int = 0, part: int = 0) -> dict:
    arg_keys = jax.random.split(jax.random.key(seed), 12)
    part_splits = jax.random.split(jax.random.fold_in(arg_keys[11], part), 12)
    features = gaussian(part_splits[0], (FRAMES, D), 1.0, 6.0, ((0, 16),))
    valid_length = jax.random.randint(part_splits[1], (1,), FRAMES // 2, FRAMES + 1).astype(jnp.int32)
    ln1_gain = jnp.clip(1.0 + 0.1 * jax.random.normal(arg_keys[2], (D,), jnp.float32), 0.5, 1.5)
    w_qkv = draw_w_qkv(jax.random.fold_in(arg_keys[11], 71), part)
    w_out = gaussian(arg_keys[4], (ATT, D), ATT ** -0.5, 0.25, ((0, 16),))
    ln2_gain = jnp.clip(1.0 + 0.1 * jax.random.normal(arg_keys[5], (D,), jnp.float32), 0.5, 1.5)
    w_pw1 = gaussian(arg_keys[6], (D, 2 * D), D ** -0.5, 0.1875, ((0, 16),))
    w_dw = gaussian(arg_keys[7], (KERNEL, D), KERNEL ** -0.5, 2.0, (), jnp.float32)
    bn_scale = jnp.clip(jnp.exp(jax.random.uniform(arg_keys[8], (D,), jnp.float32, math.log(0.5), math.log(2.0))), 0.5, 2.0)
    bn_shift = gaussian(arg_keys[9], (D,), 0.5, 3.0, (), jnp.float32)
    w_pw2 = gaussian(arg_keys[10], (D, D), D ** -0.5, 0.1875, ((0, 16),))
    return dict(features=features, valid_length=valid_length, ln1_gain=ln1_gain, w_qkv=w_qkv, w_out=w_out, ln2_gain=ln2_gain, w_pw1=w_pw1, w_dw=w_dw, bn_scale=bn_scale, bn_shift=bn_shift, w_pw2=w_pw2)


EPSILON = 1e-05

def layer_norm(values, gain):
    values = values.astype(jnp.float32)
    mean = lax.optimization_barrier(jnp.mean(values, axis=-1, keepdims=True))
    centred = values - mean
    variance = lax.optimization_barrier(jnp.mean(centred * centred, axis=-1, keepdims=True))
    return (centred * lax.rsqrt(variance + EPSILON) * gain).astype(jnp.bfloat16)

def reference(features, valid_length, ln1_gain, w_qkv, w_out, ln2_gain, w_pw1, w_dw, bn_scale, bn_shift, w_pw2):
    limit = valid_length[0]
    normed1 = layer_norm(features, ln1_gain)
    qkv = jnp.dot(normed1, w_qkv, preferred_element_type=jnp.float32).astype(jnp.bfloat16)
    queries = qkv[:, :ATT].reshape(FRAMES, HEADS, HD).transpose(1, 0, 2)
    keys = qkv[:, ATT:2 * ATT].reshape(FRAMES, HEADS, HD).transpose(1, 0, 2)
    values = qkv[:, 2 * ATT:].reshape(FRAMES, HEADS, HD).transpose(1, 0, 2)
    key_valid = (jnp.arange(FRAMES, dtype=jnp.int32) < limit)[None, :]
    scale = 1.0 / math.sqrt(HD)
    block = math.gcd(FRAMES, 512)

    def one_head(triple):
        head_q, head_k, head_v = triple
        blocks_q = head_q.reshape(FRAMES // block, block, HD)

        def one_block(query_rows):
            scores = jnp.dot(query_rows, head_k.T, preferred_element_type=jnp.float32) * scale
            scores = jnp.where(key_valid, scores, -1e+30)
            peak = lax.optimization_barrier(jnp.max(scores, axis=-1, keepdims=True))
            weights = jnp.where(key_valid, jnp.exp(scores - peak), 0.0)
            totals = lax.optimization_barrier(jnp.sum(weights, axis=-1, keepdims=True))
            summed = jnp.dot(weights.astype(jnp.bfloat16), head_v, preferred_element_type=jnp.float32)
            return summed / totals
        return lax.map(one_block, blocks_q).reshape(FRAMES, HD)
    context = lax.map(one_head, (queries, keys, values))
    context = context.transpose(1, 0, 2).reshape(FRAMES, ATT).astype(jnp.bfloat16)
    attended = features.astype(jnp.float32) + jnp.dot(context, w_out, preferred_element_type=jnp.float32)
    normed2 = layer_norm(attended, ln2_gain)
    both = jnp.dot(normed2, w_pw1, preferred_element_type=jnp.float32)
    frame_valid = (jnp.arange(FRAMES, dtype=jnp.int32) < limit)[:, None]
    gated = jnp.where(frame_valid, both[:, :D] * jax.nn.sigmoid(both[:, D:]), 0.0).astype(jnp.bfloat16)
    padded = jnp.pad(gated.astype(jnp.float32), ((HALF, HALF), (0, 0)))
    conv = jnp.zeros((FRAMES, D), jnp.float32)
    for tap in range(KERNEL):
        conv = conv + w_dw[tap][None, :] * padded[tap:tap + FRAMES]
    activated = jax.nn.silu(bn_scale * conv + bn_shift).astype(jnp.bfloat16)
    result = attended + jnp.dot(activated, w_pw2, preferred_element_type=jnp.float32)
    return result.astype(jnp.bfloat16)
```

```python
import functools
import math

import jax
import jax.numpy as jnp
from jax import lax
from jax.experimental import pallas as pl
from jax.experimental.pallas import tpu as pltpu
from jax.sharding import PartitionSpec as P

HEADS = 4
HD = 128

EPSILON = 1e-05
EDGE = 16
LOG2E = 1.4426950408889634

ORDER_EVEN = (8, 4, 2)
ORDER_ODD = (2, 8, 4)
ALONG_Z = (0, 8, 4, 12)


def extended(cells, sides, width):
    for axis, dim in sides:
        count = lax.axis_size(axis)
        ends = count - 1
        head = lax.slice_in_dim(cells, 0, width, axis=dim)
        tail = lax.slice_in_dim(cells, cells.shape[dim] - width, cells.shape[dim], axis=dim)
        cells = jnp.concatenate(
            [
                lax.ppermute(tail, axis, [(i, (i + 1) % count) for i in range(ends)]),
                cells,
                lax.ppermute(head, axis, [((i + 1) % count, i) for i in range(ends)]),
            ],
            axis=dim,
        )
    return cells


def layer_norm(values, gain):
    values = values.astype(jnp.float32)
    mean = jnp.mean(values, axis=-1, keepdims=True)
    centred = values - mean
    variance = jnp.mean(centred * centred, axis=-1, keepdims=True)
    return (centred * lax.rsqrt(variance + EPSILON) * gain).astype(jnp.bfloat16)


def per_device_general(
    features, valid_length, ln1_gain, w_qkv, w_out, ln2_gain, w_pw1, w_dw, bn_scale, bn_shift, w_pw2
):
    limit = valid_length[0]
    local_rows = features.shape[0]
    width = features.shape[1]
    att_width = w_qkv.shape[1] // 3
    scale = 1.0 / math.sqrt(HD)
    full_out = lax.all_gather(w_out, "frames", axis=0, tiled=True)
    full_pw1 = lax.all_gather(w_pw1, "frames", axis=0, tiled=True)
    full_pw2 = lax.all_gather(w_pw2, "frames", axis=0, tiled=True)
    normed1 = layer_norm(features, ln1_gain)
    qkv = jnp.dot(
        normed1,
        lax.all_gather(w_qkv, "frames", axis=0, tiled=True),
        preferred_element_type=jnp.float32,
    ).astype(jnp.bfloat16)
    query_heads = qkv[:, :att_width].reshape(local_rows, HEADS, HD)
    pairs = lax.all_gather(qkv[:, att_width:], "frames", axis=0, tiled=True)
    count = pairs.shape[0]
    key_heads = pairs[:, :att_width].reshape(count, HEADS, HD)
    value_heads = pairs[:, att_width:].reshape(count, HEADS, HD)
    scores = (
        jnp.einsum("qhd,khd->hqk", query_heads, key_heads, preferred_element_type=jnp.float32)
        * scale
    )
    valid = (jnp.arange(count, dtype=jnp.int32) < limit)[None, None, :]
    scores = jnp.where(valid, scores, -1e30)
    maxima = jnp.max(scores, axis=-1)
    weights = jnp.where(valid, jnp.exp(scores - maxima[..., None]), 0.0)
    totals = jnp.sum(weights, axis=-1)
    summed = jnp.einsum(
        "hqk,khd->hqd",
        weights.astype(jnp.bfloat16),
        value_heads,
        preferred_element_type=jnp.float32,
    )
    context = (
        (summed / totals[..., None])
        .transpose(1, 0, 2)
        .reshape(local_rows, att_width)
        .astype(jnp.bfloat16)
    )
    attended = features.astype(jnp.float32) + jnp.dot(
        context, full_out, preferred_element_type=jnp.float32
    )
    normed2 = layer_norm(attended, ln2_gain)
    both = jnp.dot(normed2, full_pw1, preferred_element_type=jnp.float32)
    frame_index = lax.axis_index("frames") * local_rows + jnp.arange(local_rows, dtype=jnp.int32)
    frame_valid = (frame_index < limit)[:, None]
    gated = jnp.where(frame_valid, both[:, :width] * jax.nn.sigmoid(both[:, width:]), 0.0).astype(
        jnp.bfloat16
    )
    half_window = (w_dw.shape[0] - 1) // 2
    widened = extended(gated, (("frames", 0),), half_window).astype(jnp.float32)
    conv = jnp.zeros((local_rows, width), jnp.float32)
    for tap in range(w_dw.shape[0]):
        conv = conv + w_dw[tap][None, :] * widened[tap : tap + local_rows]
    activated = jax.nn.silu(bn_scale * conv + bn_shift).astype(jnp.bfloat16)
    result = attended + jnp.dot(activated, full_pw2, preferred_element_type=jnp.float32)
    return result.astype(jnp.bfloat16)


def swap(array, even, odd=None):
    odd = even if odd is None else odd
    pairs = [(i, i ^ (odd if i & 1 else even)) for i in range(16)]
    return lax.ppermute(array, "frames", pairs)


def block_masks(order):
    masks = [0]
    for bit in order:
        masks = masks + [mask ^ bit for mask in masks]
    return masks


def after(arrays, others):
    joined = lax.optimization_barrier(tuple(arrays) + tuple(others))
    return joined[: len(arrays)]


def source_of(me, j, even, odd, other_core):
    origin = me ^ 1 if other_core else me
    core = origin & 1
    return origin ^ jnp.where(core == 0, even[j], odd[j])


def attention_kernel(
    scalars, own_x, other_x, own_w, other_w, *refs, rows, even, odd, w_masks, count
):
    outs, (x_all, w_all, keys, values, sems) = refs[:4], refs[4:]
    me, limit = scalars[0], scalars[1]
    depth = w_all.shape[0] // 16
    for other_core, (xs, ws) in enumerate(((own_x, own_w), (other_x, other_w))):
        for j in range(8):
            src = source_of(me, j, w_masks, w_masks, other_core)
            pltpu.make_async_copy(
                ws.at[pl.ds(j * depth, depth)],
                w_all.at[pl.ds(pl.multiple_of(src * depth, depth), depth)],
                sems.at[0],
            ).start()
        for j in range(8):
            src = source_of(me, j, even, odd, other_core)
            pltpu.make_async_copy(
                xs.at[pl.ds(j * rows, rows)],
                x_all.at[pl.ds(pl.multiple_of(EDGE + src * rows, EDGE), rows)],
                sems.at[1],
            ).start()
    width = x_all.shape[1]
    x_all[0:EDGE, :] = jnp.zeros((EDGE, width), jnp.bfloat16)
    x_all[EDGE + count : 2 * EDGE + count, :] = jnp.zeros((EDGE, width), jnp.bfloat16)
    pltpu.make_async_copy(w_all, w_all, sems.at[0]).wait()
    inner = x_all.at[pl.ds(EDGE, count)]
    pltpu.make_async_copy(inner, inner, sems.at[1]).wait()
    step = 512
    for r in range(count // step):
        both = jnp.dot(
            x_all[EDGE + r * step : EDGE + (r + 1) * step, :],
            w_all[:, HD:],
            preferred_element_type=jnp.float32,
        ).astype(jnp.bfloat16)
        keys[r * step : (r + 1) * step, :] = both[:, :HD]
        values[r * step : (r + 1) * step, :] = both[:, HD:]
    wide = rows + 2 * EDGE
    position = lax.broadcasted_iota(jnp.int32, (1, count), 1)
    valid = position < limit
    factor = LOG2E / math.sqrt(HD)
    for mask, out in zip(ALONG_Z, outs):
        start = pl.multiple_of((me ^ mask) * rows, EDGE)
        query = jnp.dot(
            x_all[pl.ds(start, wide), :], w_all[:, :HD], preferred_element_type=jnp.float32
        ).astype(jnp.bfloat16)
        scores = lax.dot_general(
            query, keys[...], (((1,), (1,)), ((), ())), preferred_element_type=jnp.float32
        )
        scores = jnp.where(valid, scores * factor, -1e30)
        weights = jnp.exp2(scores - jnp.max(scores, axis=-1, keepdims=True))
        totals = jnp.sum(weights, axis=-1, keepdims=True)
        summed = jnp.dot(
            weights.astype(jnp.bfloat16), values[...], preferred_element_type=jnp.float32
        )
        out[...] = (summed / totals).astype(jnp.bfloat16)


def tail_kernel(
    scalars, c0, c1, c2, c3, feats, gain, taps, bn_scale, bn_shift, own, other, out,
    w_out, w_value, w_gate, w_last, wide_gated, sems, *, rows, even, odd, parts
):
    me, limit = scalars[0], scalars[1]
    size = sum(parts)
    homes = (w_out, w_value, w_gate, w_last)
    starts = [sum(parts[:i]) for i in range(len(parts))]
    for i, home in enumerate(homes):
        for other_core, held in enumerate((own, other)):
            for j in range(8):
                src = source_of(me, j, even, odd, other_core)
                pltpu.make_async_copy(
                    held.at[pl.ds(j * size + starts[i], parts[i])],
                    home.at[pl.ds(pl.multiple_of(src * parts[i], parts[i]), parts[i])],
                    sems.at[i],
                ).start()
    wide = rows + 2 * EDGE
    attended = feats[...].astype(jnp.float32)
    head = me // 4
    pltpu.make_async_copy(w_out, w_out, sems.at[0]).wait()
    for mask, part in zip(ALONG_Z, (c0, c1, c2, c3)):
        start = pl.multiple_of((head ^ (mask // 4)) * HD, HD)
        attended = attended + jnp.dot(
            part[...], w_out[pl.ds(start, HD), :], preferred_element_type=jnp.float32
        )
    mean = jnp.mean(attended, axis=-1, keepdims=True)
    centred = attended - mean
    variance = jnp.mean(centred * centred, axis=-1, keepdims=True)
    normed2 = (centred * lax.rsqrt(variance + EPSILON) * gain[...]).astype(jnp.bfloat16)
    pltpu.make_async_copy(w_value, w_value, sems.at[1]).wait()
    value = jnp.dot(normed2, w_value[...], preferred_element_type=jnp.float32)
    pltpu.make_async_copy(w_gate, w_gate, sems.at[2]).wait()
    gate = jnp.dot(normed2, w_gate[...], preferred_element_type=jnp.float32)
    frame = me * rows - EDGE + lax.broadcasted_iota(jnp.int32, (wide, 1), 0)
    inside = (frame >= 0) & (frame < limit)
    gated = jnp.where(inside, value * jax.nn.sigmoid(gate), 0.0)
    wide_gated[...] = gated.astype(jnp.bfloat16).astype(jnp.float32)
    half = (taps.shape[0] - 1) // 2
    conv = jnp.zeros((rows, out.shape[1]), jnp.float32)
    for tap in range(taps.shape[0]):
        at = EDGE - half + tap
        conv = conv + taps[tap : tap + 1, :] * wide_gated[at : at + rows, :]
    act = bn_scale[...] * conv + bn_shift[...]
    activated = (act * jax.nn.sigmoid(act)).astype(jnp.bfloat16)
    pltpu.make_async_copy(w_last, w_last, sems.at[3]).wait()
    result = attended[EDGE : EDGE + rows, :] + jnp.dot(
        activated, w_last[...], preferred_element_type=jnp.float32
    )
    out[...] = result.astype(jnp.bfloat16)


def per_device(
    features, valid_length, ln1_gain, w_qkv, w_out, ln2_gain, w_pw1, w_dw, bn_scale, bn_shift, w_pw2
):
    rows, width = features.shape
    count = rows * 16
    depth = w_qkv.shape[0]
    me = lax.axis_index("frames")
    z = me // 4
    scalars = jnp.stack([me.astype(jnp.int32), valid_length[0]])
    even, odd = block_masks(ORDER_EVEN), block_masks(ORDER_ODD)

    normed1 = layer_norm(features, ln1_gain)
    by_head = w_qkv.reshape(depth, 3, HEADS, HD).transpose(2, 0, 1, 3).reshape(HEADS, depth, 3 * HD)
    pack = jnp.concatenate([w_out, w_pw1[:, :width], w_pw1[:, width:], w_pw2], axis=0)
    parts = (w_out.shape[0], depth, depth, depth)

    x1 = swap(normed1, ORDER_EVEN[0], ORDER_ODD[0])
    w_z = [
        swap(lax.dynamic_index_in_dim(by_head, z ^ (mask // 4), 0, keepdims=False), mask)
        for mask in ALONG_Z[1:]
    ]
    w_mine = lax.dynamic_index_in_dim(by_head, z, 0, keepdims=False)
    ahead = lax.ppermute(features[-EDGE:], "frames", [(i, i + 1) for i in range(15)])
    behind = lax.ppermute(features[:EDGE], "frames", [(i + 1, i) for i in range(15)])
    p1 = swap(pack, ORDER_EVEN[0], ORDER_ODD[0])
    x = jnp.concatenate([normed1, x1], axis=0)
    w4 = jnp.concatenate([w_mine] + w_z, axis=0)
    pack = jnp.concatenate([pack, p1], axis=0)

    x2 = swap(x, ORDER_EVEN[1], ORDER_ODD[1])
    w2 = swap(w4, 2)
    p2 = swap(pack, ORDER_EVEN[1], ORDER_ODD[1])
    x = jnp.concatenate([x, x2], axis=0)
    w8 = jnp.concatenate([w4, w2], axis=0)
    pack = jnp.concatenate([pack, p2], axis=0)

    x3 = swap(x, ORDER_EVEN[2], ORDER_ODD[2])
    w_other = swap(w8, 1)
    x = jnp.concatenate([x, x3], axis=0)
    x_other = swap(x, 1)
    p3 = swap(pack, ORDER_EVEN[2], ORDER_ODD[2])
    pack = jnp.concatenate([pack, p3], axis=0)
    pack_other = swap(pack, 1)

    wide = rows + 2 * EDGE
    w_masks = block_masks((8, 4, 2))
    any_spec = pl.BlockSpec(memory_space=pl.ANY)
    smem = pl.BlockSpec(memory_space=pltpu.SMEM)
    vmem = pl.BlockSpec(memory_space=pltpu.VMEM)
    contexts = pl.pallas_call(
        functools.partial(
            attention_kernel, rows=rows, even=even, odd=odd, w_masks=w_masks, count=count
        ),
        name="attention",
        out_shape=[jax.ShapeDtypeStruct((wide, HD), jnp.bfloat16)] * 4,
        in_specs=[smem] + [any_spec] * 4,
        out_specs=[vmem] * 4,
        scratch_shapes=[
            pltpu.VMEM((count + 2 * EDGE, width), jnp.bfloat16),
            pltpu.VMEM((16 * depth, 3 * HD), jnp.bfloat16),
            pltpu.VMEM((count, HD), jnp.bfloat16),
            pltpu.VMEM((count, HD), jnp.bfloat16),
            pltpu.SemaphoreType.DMA((2,)),
        ],
        compiler_params=pltpu.CompilerParams(vmem_limit_bytes=40 << 20),
        cost_estimate=pl.CostEstimate(
            flops=4_000_000_000, bytes_accessed=8 << 20, transcendentals=4 * wide * count
        ),
    )(scalars, x, x_other, w8, w_other)
    mine = [contexts[0]] + [swap(part, mask) for part, mask in zip(contexts[1:], ALONG_Z[1:])]

    feats = jnp.concatenate([ahead, features, behind], axis=0)
    return pl.pallas_call(
        functools.partial(tail_kernel, rows=rows, even=even, odd=odd, parts=parts),
        name="tail",
        out_shape=jax.ShapeDtypeStruct((rows, width), jnp.bfloat16),
        in_specs=[smem] + [vmem] * 9 + [any_spec] * 2,
        out_specs=vmem,
        scratch_shapes=[
            pltpu.VMEM((16 * parts[0], width), jnp.bfloat16),
            pltpu.VMEM((16 * depth, width), jnp.bfloat16),
            pltpu.VMEM((16 * depth, width), jnp.bfloat16),
            pltpu.VMEM((16 * depth, width), jnp.bfloat16),
            pltpu.VMEM((wide, width), jnp.float32),
            pltpu.SemaphoreType.DMA((4,)),
        ],
        compiler_params=pltpu.CompilerParams(vmem_limit_bytes=40 << 20),
        cost_estimate=pl.CostEstimate(
            flops=1_200_000_000, bytes_accessed=8 << 20, transcendentals=wide * width * 2
        ),
    )(
        scalars,
        *mine,
        feats,
        ln2_gain.reshape(1, -1),
        w_dw,
        bn_scale.reshape(1, -1),
        bn_shift.reshape(1, -1),
        pack,
        pack_other,
    )


def solution(mesh):
    placed = (
        P(("groups", "frames"), None),
        P("groups"),
        P(),
        P("frames", None),
        P("frames", None),
        P(),
        P("frames", None),
        P(),
        P(),
        P(),
        P("frames", None),
    )
    return jax.shard_map(
        per_device if mesh.shape["frames"] == 16 else per_device_general,
        mesh=mesh,
        in_specs=placed,
        out_specs=P(("groups", "frames"), None),
        check_vma=False,
    )
```

```python
import functools
import math

import jax
import jax.numpy as jnp
from jax import lax
from jax.experimental import pallas as pl
from jax.experimental.pallas import tpu as pltpu
from jax.sharding import PartitionSpec as P

HEADS = 4
HD = 128

EPSILON = 1e-05
EDGE = 16
LOG2E = 1.4426950408889634

ORDER_EVEN = (8, 4, 2)
ORDER_ODD = (2, 8, 4)
PACK_EVEN = (8, 4, 2, 16)
PACK_ODD = (8, 2, 16, 4)
ALONG_Z = (0, 8, 4, 12)


def extended(cells, sides, width):
    for axis, dim in sides:
        count = lax.axis_size(axis)
        ends = count - 1
        head = lax.slice_in_dim(cells, 0, width, axis=dim)
        tail = lax.slice_in_dim(cells, cells.shape[dim] - width, cells.shape[dim], axis=dim)
        cells = jnp.concatenate(
            [
                lax.ppermute(tail, axis, [(i, (i + 1) % count) for i in range(ends)]),
                cells,
                lax.ppermute(head, axis, [((i + 1) % count, i) for i in range(ends)]),
            ],
            axis=dim,
        )
    return cells


def layer_norm(values, gain):
    values = values.astype(jnp.float32)
    mean = jnp.mean(values, axis=-1, keepdims=True)
    centred = values - mean
    variance = jnp.mean(centred * centred, axis=-1, keepdims=True)
    return (centred * lax.rsqrt(variance + EPSILON) * gain).astype(jnp.bfloat16)


def per_device_general(
    features, valid_length, ln1_gain, w_qkv, w_out, ln2_gain, w_pw1, w_dw, bn_scale, bn_shift, w_pw2
):
    limit = valid_length[0]
    local_rows = features.shape[0]
    width = features.shape[1]
    att_width = w_qkv.shape[1] // 3
    scale = 1.0 / math.sqrt(HD)
    full_out = lax.all_gather(w_out, "frames", axis=0, tiled=True)
    full_pw1 = lax.all_gather(w_pw1, "frames", axis=0, tiled=True)
    full_pw2 = lax.all_gather(w_pw2, "frames", axis=0, tiled=True)
    normed1 = layer_norm(features, ln1_gain)
    qkv = jnp.dot(
        normed1,
        lax.all_gather(w_qkv, "frames", axis=0, tiled=True),
        preferred_element_type=jnp.float32,
    ).astype(jnp.bfloat16)
    query_heads = qkv[:, :att_width].reshape(local_rows, HEADS, HD)
    pairs = lax.all_gather(qkv[:, att_width:], "frames", axis=0, tiled=True)
    count = pairs.shape[0]
    key_heads = pairs[:, :att_width].reshape(count, HEADS, HD)
    value_heads = pairs[:, att_width:].reshape(count, HEADS, HD)
    scores = (
        jnp.einsum("qhd,khd->hqk", query_heads, key_heads, preferred_element_type=jnp.float32)
        * scale
    )
    valid = (jnp.arange(count, dtype=jnp.int32) < limit)[None, None, :]
    scores = jnp.where(valid, scores, -1e30)
    maxima = jnp.max(scores, axis=-1)
    weights = jnp.where(valid, jnp.exp(scores - maxima[..., None]), 0.0)
    totals = jnp.sum(weights, axis=-1)
    summed = jnp.einsum(
        "hqk,khd->hqd",
        weights.astype(jnp.bfloat16),
        value_heads,
        preferred_element_type=jnp.float32,
    )
    context = (
        (summed / totals[..., None])
        .transpose(1, 0, 2)
        .reshape(local_rows, att_width)
        .astype(jnp.bfloat16)
    )
    attended = features.astype(jnp.float32) + jnp.dot(
        context, full_out, preferred_element_type=jnp.float32
    )
    normed2 = layer_norm(attended, ln2_gain)
    both = jnp.dot(normed2, full_pw1, preferred_element_type=jnp.float32)
    frame_index = lax.axis_index("frames") * local_rows + jnp.arange(local_rows, dtype=jnp.int32)
    frame_valid = (frame_index < limit)[:, None]
    gated = jnp.where(frame_valid, both[:, :width] * jax.nn.sigmoid(both[:, width:]), 0.0).astype(
        jnp.bfloat16
    )
    half_window = (w_dw.shape[0] - 1) // 2
    widened = extended(gated, (("frames", 0),), half_window).astype(jnp.float32)
    conv = jnp.zeros((local_rows, width), jnp.float32)
    for tap in range(w_dw.shape[0]):
        conv = conv + w_dw[tap][None, :] * widened[tap : tap + local_rows]
    activated = jax.nn.silu(bn_scale * conv + bn_shift).astype(jnp.bfloat16)
    result = attended + jnp.dot(activated, full_pw2, preferred_element_type=jnp.float32)
    return result.astype(jnp.bfloat16)


def swap(array, even, odd=None, groups=None):
    odd = even if odd is None else odd
    if groups is None:
        pairs = [(i, i ^ (odd if i & 1 else even)) for i in range(16)]
        return lax.ppermute(array, "frames", pairs)
    pairs = [(i, i ^ (odd if i & 1 else even)) for i in range(16 * groups)]
    return lax.ppermute(array, ("groups", "frames"), pairs)


def block_masks(order):
    masks = [0]
    for bit in order:
        masks = masks + [mask ^ bit for mask in masks]
    return masks


def source_of(me, j, even, odd, other_core):
    origin = me ^ 1 if other_core else me
    core = origin & 1
    return origin ^ jnp.where(core == 0, even[j], odd[j])


def prepare_kernel(
    scalars, feats_in, gain, w_qkv, w_out, w_pw1, w_pw2, normed, head0, head1, head2, head3, pack, feats, sems
):
    me, group = scalars[0], scalars[3]
    load = pltpu.make_async_copy(feats_in, feats, sems.at[0])
    load.start()
    att = w_qkv.shape[1] // 3
    width = feats.shape[1]
    copies = []
    for mask, out in zip(ALONG_Z, (head0, head1, head2, head3)):
        head = (me ^ mask) // 4
        for i in range(3):
            start = pl.multiple_of(i * att + head * HD, HD)
            copies.append((w_qkv.at[:, pl.ds(start, HD)], out.at[:, i * HD : (i + 1) * HD]))
    half = pack.shape[0]
    start = pl.multiple_of(group * half, half)
    copies.append((w_pw1.at[pl.ds(start, half)], pack.at[:, 0 : 2 * width]))
    copies.append((w_pw2.at[pl.ds(start, half)], pack.at[:, 2 * width : 3 * width]))
    side = pl.multiple_of(group * (width // 2), width // 2)
    copies.append((w_out.at[:, pl.ds(side, width // 2)], pack.at[:, 3 * width :]))
    copies = [pltpu.make_async_copy(a, b, sems.at[1 + i]) for i, (a, b) in enumerate(copies)]
    for copy in copies:
        copy.start()
    load.wait()
    values = feats[...].astype(jnp.float32)
    mean = jnp.mean(values, axis=-1, keepdims=True)
    centred = values - mean
    variance = jnp.mean(centred * centred, axis=-1, keepdims=True)
    normed[...] = (centred * lax.rsqrt(variance + EPSILON) * gain[...]).astype(jnp.bfloat16)
    for copy in copies:
        copy.wait()


def attention_kernel(
    scalars, xa, xb, xa_other, xb_other, own_w, other_w, *refs, rows, even, odd, w_masks, count
):
    outs, (x_all, w_all, keys, values, sems) = refs[:4], refs[4:]
    me, limit = scalars[0], scalars[1]
    depth = w_all.shape[0] // 16
    for other_core, (xs, ws) in enumerate((((xa, xb), own_w), ((xa_other, xb_other), other_w))):
        for j in range(8):
            src = source_of(me, j, w_masks, w_masks, other_core)
            pltpu.make_async_copy(
                ws.at[pl.ds(j * depth, depth)],
                w_all.at[pl.ds(pl.multiple_of(src * depth, depth), depth)],
                sems.at[0],
            ).start()
        for j in range(8):
            src = source_of(me, j, even, odd, other_core)
            pltpu.make_async_copy(
                xs[j // 4].at[pl.ds((j % 4) * rows, rows)],
                x_all.at[pl.ds(pl.multiple_of(EDGE + src * rows, EDGE), rows)],
                sems.at[1],
            ).start()
    width = x_all.shape[1]
    x_all[0:EDGE, :] = jnp.zeros((EDGE, width), jnp.bfloat16)
    x_all[EDGE + count : 2 * EDGE + count, :] = jnp.zeros((EDGE, width), jnp.bfloat16)
    pltpu.make_async_copy(w_all, w_all, sems.at[0]).wait()
    inner = x_all.at[pl.ds(EDGE, count)]
    pltpu.make_async_copy(inner, inner, sems.at[1]).wait()
    step = 512
    for r in range(count // step):
        both = jnp.dot(
            x_all[EDGE + r * step : EDGE + (r + 1) * step, :],
            w_all[:, HD:],
            preferred_element_type=jnp.float32,
        ).astype(jnp.bfloat16)
        keys[r * step : (r + 1) * step, :] = both[:, :HD]
        values[r * step : (r + 1) * step, :] = both[:, HD:]
    wide = rows + 2 * EDGE
    position = lax.broadcasted_iota(jnp.int32, (1, count), 1)
    valid = position < limit
    factor = LOG2E / math.sqrt(HD)
    for mask, out in zip(ALONG_Z, outs):
        start = pl.multiple_of((me ^ mask) * rows, EDGE)
        query = jnp.dot(
            x_all[pl.ds(start, wide), :], w_all[:, :HD], preferred_element_type=jnp.float32
        ).astype(jnp.bfloat16)
        scores = lax.dot_general(
            query, keys[...], (((1,), (1,)), ((), ())), preferred_element_type=jnp.float32
        )
        scores = jnp.where(valid, scores * factor, -1e30)
        weights = jnp.exp2(scores - jnp.max(scores, axis=-1, keepdims=True))
        totals = jnp.sum(weights, axis=-1, keepdims=True)
        summed = jnp.dot(
            weights.astype(jnp.bfloat16), values[...], preferred_element_type=jnp.float32
        )
        out[...] = (summed / totals).astype(jnp.bfloat16)


def bit_of(number, position):
    return (number >> position) & 1


def lane_sources(place, lanes, step):
    block = (lanes % (lanes.shape[1] // 2)) // step
    other = lanes // (lanes.shape[1] // 2)
    origin = place ^ other
    core = origin & 1
    for i, (even, odd) in enumerate(zip(PACK_EVEN, PACK_ODD)):
        origin = origin ^ (bit_of(block, i) * jnp.where(core == 0, even, odd))
    return origin


def tail_kernel(
    scalars, c0, c1, c2, c3, feats, gain, taps, bn_scale, bn_shift, pa, pb, pa_other, pb_other, out,
    v0, v1, v2, v3, wide_gated, sems, *, rows
):
    me, limit, place = scalars[0], scalars[1], scalars[2]
    held = (v0, v1, v2, v3)
    copies = [
        pltpu.make_async_copy(a, b, sems.at[i])
        for i, (a, b) in enumerate(zip((pa, pa_other, pb, pb_other), (v0, v2, v1, v3)))
    ]
    for copy in copies:
        copy.start()
    wide = rows + 2 * EDGE
    width = out.shape[1]
    quarter = width // 4
    step = v0.shape[0] // 8
    lanes = lax.broadcasted_iota(jnp.int32, (1, width), 1)
    source = lane_sources(place, lanes, step)
    index = (source & 15) * (2 * step) + (source // 16) * step + lanes % step
    line = lax.broadcasted_iota(jnp.int32, (width, width), 0)
    mixing = jnp.where(line == index, 1.0, 0.0).astype(jnp.bfloat16)

    def mixed(array, by):
        return jnp.dot(array, by, preferred_element_type=jnp.float32).astype(jnp.bfloat16)

    def times(array, start, stop):
        total = None
        for i, part in enumerate(held):
            term = jnp.dot(
                array[:, i * quarter : (i + 1) * quarter],
                part[:, start:stop],
                preferred_element_type=jnp.float32,
            )
            total = term if total is None else total + term
        return total

    row_out = (source & 15) * step + lanes % step
    side = source // 16
    heads = [((me ^ mask) // 4) for mask in ALONG_Z]
    halves = []
    spreads = [0.0, 0.0]
    small = lax.broadcasted_iota(jnp.int32, (HD, width), 0)
    for head, part in zip(heads, (c0, c1, c2, c3)):
        for h in range(2):
            by = jnp.where((small + head * HD == row_out) & (side == h), 1.0, 0.0).astype(jnp.bfloat16)
            spreads[h] = spreads[h] + jnp.dot(part[...], by, preferred_element_type=jnp.float32)
    for copy in copies:
        copy.wait()
    for h in range(2):
        halves.append(times(spreads[h].astype(jnp.bfloat16), 3 * width, 3 * width + width // 2))
    attended = feats[...].astype(jnp.float32) + jnp.concatenate(halves, axis=1)
    mean = jnp.mean(attended, axis=-1, keepdims=True)
    centred = attended - mean
    variance = jnp.mean(centred * centred, axis=-1, keepdims=True)
    normed2 = (centred * lax.rsqrt(variance + EPSILON) * gain[...]).astype(jnp.bfloat16)
    normed2 = mixed(normed2, mixing)
    value = times(normed2, 0, width)
    gate = times(normed2, width, 2 * width)
    frame = me * rows - EDGE + lax.broadcasted_iota(jnp.int32, (wide, 1), 0)
    inside = (frame >= 0) & (frame < limit)
    gated = jnp.where(inside, value * jax.nn.sigmoid(gate), 0.0)
    wide_gated[...] = gated.astype(jnp.bfloat16).astype(jnp.float32)
    half = (taps.shape[0] - 1) // 2
    conv = jnp.zeros((rows, out.shape[1]), jnp.float32)
    for tap in range(taps.shape[0]):
        at = EDGE - half + tap
        conv = conv + taps[tap : tap + 1, :] * wide_gated[at : at + rows, :]
    act = bn_scale[...] * conv + bn_shift[...]
    activated = (act * jax.nn.sigmoid(act)).astype(jnp.bfloat16)
    result = attended[EDGE : EDGE + rows, :] + times(mixed(activated, mixing), 2 * width, 3 * width)
    out[...] = result.astype(jnp.bfloat16)


def per_device(
    features, valid_length, ln1_gain, w_qkv, w_out, ln2_gain, w_pw1, w_dw, bn_scale, bn_shift, w_pw2
):
    rows, width = features.shape
    count = rows * 16
    depth = w_qkv.shape[0]
    me = lax.axis_index("frames")
    group = lax.axis_index("groups")
    groups = lax.axis_size("groups")
    scalars = jnp.stack([me, valid_length[0], 16 * group + me, group]).astype(jnp.int32)
    even, odd = block_masks(ORDER_EVEN), block_masks(ORDER_ODD)
    any_spec = pl.BlockSpec(memory_space=pl.ANY)
    hbm = pl.BlockSpec(memory_space=pltpu.HBM)
    smem = pl.BlockSpec(memory_space=pltpu.SMEM)
    vmem = pl.BlockSpec(memory_space=pltpu.VMEM)

    normed1, w_mine, w_8, w_4, w_12, pack = pl.pallas_call(
        prepare_kernel,
        name="prepare",
        out_shape=[jax.ShapeDtypeStruct((rows, width), jnp.bfloat16)]
        + [jax.ShapeDtypeStruct((depth, 3 * HD), jnp.bfloat16)] * 4
        + [jax.ShapeDtypeStruct((depth // 2, 3 * width + width // 2), jnp.bfloat16)],
        in_specs=[smem, hbm, vmem] + [hbm] * 4,
        out_specs=[vmem] * 6,
        scratch_shapes=[
            pltpu.VMEM((rows, width), jnp.bfloat16),
            pltpu.SemaphoreType.DMA((16,)),
        ],
        compiler_params=pltpu.CompilerParams(vmem_limit_bytes=16 << 20),
    )(scalars, features, ln1_gain.reshape(1, -1), w_qkv, w_out, w_pw1, w_pw2)

    def joined(*arrays):
        return lax.optimization_barrier(jnp.concatenate(arrays, axis=0))

    def pack_swap(held, stage):
        return swap(held, PACK_EVEN[stage], PACK_ODD[stage], groups)

    ahead = lax.ppermute(features[-EDGE:], "frames", [(i, i + 1) for i in range(15)])
    behind = lax.ppermute(features[:EDGE], "frames", [(i + 1, i) for i in range(15)])
    x1 = swap(normed1, ORDER_EVEN[0], ORDER_ODD[0])
    w_z = [swap(part, mask) for part, mask in zip((w_8, w_4, w_12), ALONG_Z[1:])]
    p2 = joined(pack, pack_swap(pack, 0))
    x2 = joined(normed1, x1)
    w4 = joined(w_mine, *w_z)
    x2, w4, ahead, behind = lax.optimization_barrier((x2, w4, ahead, behind))

    w8 = joined(w4, swap(w4, 2))
    p4 = joined(p2, pack_swap(p2, 1))
    xa = joined(x2, swap(x2, ORDER_EVEN[1], ORDER_ODD[1]))
    xa, w8 = lax.optimization_barrier((xa, w8))

    xb = swap(xa, ORDER_EVEN[2], ORDER_ODD[2])
    xa_other = swap(xa, 1)
    w_other = swap(w8, 1)
    pa = joined(p4, pack_swap(p4, 2))
    xb, xa_other, w_other = lax.optimization_barrier((xb, xa_other, w_other))
    xb_other = swap(xb, 1)
    pb = pack_swap(pa, 3)
    pa_other = swap(pa, 1)

    wide = rows + 2 * EDGE
    w_masks = block_masks((8, 4, 2))
    contexts = pl.pallas_call(
        functools.partial(
            attention_kernel, rows=rows, even=even, odd=odd, w_masks=w_masks, count=count
        ),
        name="attention",
        out_shape=[jax.ShapeDtypeStruct((wide, HD), jnp.bfloat16)] * 4,
        in_specs=[smem] + [any_spec] * 6,
        out_specs=[vmem] * 4,
        scratch_shapes=[
            pltpu.VMEM((count + 2 * EDGE, width), jnp.bfloat16),
            pltpu.VMEM((16 * depth, 3 * HD), jnp.bfloat16),
            pltpu.VMEM((count, HD), jnp.bfloat16),
            pltpu.VMEM((count, HD), jnp.bfloat16),
            pltpu.SemaphoreType.DMA((2,)),
        ],
        compiler_params=pltpu.CompilerParams(vmem_limit_bytes=40 << 20),
        cost_estimate=pl.CostEstimate(
            flops=5_000_000_000, bytes_accessed=8 << 20, transcendentals=4 * wide * count
        ),
    )(scalars, xa, xb, xa_other, xb_other, w8, w_other)
    pb, contexts = lax.optimization_barrier((pb, contexts))
    pb_other = swap(pb, 1)
    mine = [contexts[0]] + [swap(part, mask) for part, mask in zip(contexts[1:], ALONG_Z[1:])]

    feats = jnp.concatenate([ahead, features, behind], axis=0)
    return pl.pallas_call(
        functools.partial(tail_kernel, rows=rows),
        name="tail",
        out_shape=jax.ShapeDtypeStruct((rows, width), jnp.bfloat16),
        in_specs=[smem] + [vmem] * 9 + [any_spec] * 4,
        out_specs=vmem,
        scratch_shapes=[
            pltpu.VMEM(pa.shape, jnp.bfloat16),
            pltpu.VMEM(pa.shape, jnp.bfloat16),
            pltpu.VMEM(pa.shape, jnp.bfloat16),
            pltpu.VMEM(pa.shape, jnp.bfloat16),
            pltpu.VMEM((wide, width), jnp.float32),
            pltpu.SemaphoreType.DMA((4,)),
        ],
        compiler_params=pltpu.CompilerParams(vmem_limit_bytes=40 << 20),
        cost_estimate=pl.CostEstimate(
            flops=1_200_000_000, bytes_accessed=8 << 20, transcendentals=wide * width * 2
        ),
    )(
        scalars,
        *mine,
        feats,
        ln2_gain.reshape(1, -1),
        w_dw,
        bn_scale.reshape(1, -1),
        bn_shift.reshape(1, -1),
        pa,
        pb,
        pa_other,
        pb_other,
    )


def solution(mesh):
    placed = (
        P(("groups", "frames"), None),
        P("groups"),
        P(),
        P("frames", None),
        P("frames", None),
        P(),
        P("frames", None),
        P(),
        P(),
        P(),
        P("frames", None),
    )
    return jax.shard_map(
        per_device if (mesh.shape["groups"], mesh.shape["frames"]) == (2, 16) else per_device_general,
        mesh=mesh,
        in_specs=placed,
        out_specs=P(("groups", "frames"), None),
        check_vma=False,
    )
```

```python
import functools
import math

import jax
import jax.numpy as jnp
from jax import lax
from jax.experimental import pallas as pl
from jax.experimental.pallas import tpu as pltpu
from jax.sharding import PartitionSpec as P

HEADS = 4
HD = 128

EPSILON = 1e-05
EDGE = 16
LOG2E = 1.4426950408889634

ORDER_EVEN = (8, 4, 2)
ORDER_ODD = (2, 8, 4)
PACK_EVEN = (8, 4, 2, 16)
PACK_ODD = (8, 2, 16, 4)
ALONG_Z = (0, 8, 4, 12)


def extended(cells, sides, width):
    for axis, dim in sides:
        count = lax.axis_size(axis)
        ends = count - 1
        head = lax.slice_in_dim(cells, 0, width, axis=dim)
        tail = lax.slice_in_dim(cells, cells.shape[dim] - width, cells.shape[dim], axis=dim)
        cells = jnp.concatenate(
            [
                lax.ppermute(tail, axis, [(i, (i + 1) % count) for i in range(ends)]),
                cells,
                lax.ppermute(head, axis, [((i + 1) % count, i) for i in range(ends)]),
            ],
            axis=dim,
        )
    return cells


def layer_norm(values, gain):
    values = values.astype(jnp.float32)
    mean = jnp.mean(values, axis=-1, keepdims=True)
    centred = values - mean
    variance = jnp.mean(centred * centred, axis=-1, keepdims=True)
    return (centred * lax.rsqrt(variance + EPSILON) * gain).astype(jnp.bfloat16)


def per_device_general(
    features, valid_length, ln1_gain, w_qkv, w_out, ln2_gain, w_pw1, w_dw, bn_scale, bn_shift, w_pw2
):
    limit = valid_length[0]
    local_rows = features.shape[0]
    width = features.shape[1]
    att_width = w_qkv.shape[1] // 3
    scale = 1.0 / math.sqrt(HD)
    full_out = lax.all_gather(w_out, "frames", axis=0, tiled=True)
    full_pw1 = lax.all_gather(w_pw1, "frames", axis=0, tiled=True)
    full_pw2 = lax.all_gather(w_pw2, "frames", axis=0, tiled=True)
    normed1 = layer_norm(features, ln1_gain)
    qkv = jnp.dot(
        normed1,
        lax.all_gather(w_qkv, "frames", axis=0, tiled=True),
        preferred_element_type=jnp.float32,
    ).astype(jnp.bfloat16)
    query_heads = qkv[:, :att_width].reshape(local_rows, HEADS, HD)
    pairs = lax.all_gather(qkv[:, att_width:], "frames", axis=0, tiled=True)
    count = pairs.shape[0]
    key_heads = pairs[:, :att_width].reshape(count, HEADS, HD)
    value_heads = pairs[:, att_width:].reshape(count, HEADS, HD)
    scores = (
        jnp.einsum("qhd,khd->hqk", query_heads, key_heads, preferred_element_type=jnp.float32)
        * scale
    )
    valid = (jnp.arange(count, dtype=jnp.int32) < limit)[None, None, :]
    scores = jnp.where(valid, scores, -1e30)
    maxima = jnp.max(scores, axis=-1)
    weights = jnp.where(valid, jnp.exp(scores - maxima[..., None]), 0.0)
    totals = jnp.sum(weights, axis=-1)
    summed = jnp.einsum(
        "hqk,khd->hqd",
        weights.astype(jnp.bfloat16),
        value_heads,
        preferred_element_type=jnp.float32,
    )
    context = (
        (summed / totals[..., None])
        .transpose(1, 0, 2)
        .reshape(local_rows, att_width)
        .astype(jnp.bfloat16)
    )
    attended = features.astype(jnp.float32) + jnp.dot(
        context, full_out, preferred_element_type=jnp.float32
    )
    normed2 = layer_norm(attended, ln2_gain)
    both = jnp.dot(normed2, full_pw1, preferred_element_type=jnp.float32)
    frame_index = lax.axis_index("frames") * local_rows + jnp.arange(local_rows, dtype=jnp.int32)
    frame_valid = (frame_index < limit)[:, None]
    gated = jnp.where(frame_valid, both[:, :width] * jax.nn.sigmoid(both[:, width:]), 0.0).astype(
        jnp.bfloat16
    )
    half_window = (w_dw.shape[0] - 1) // 2
    widened = extended(gated, (("frames", 0),), half_window).astype(jnp.float32)
    conv = jnp.zeros((local_rows, width), jnp.float32)
    for tap in range(w_dw.shape[0]):
        conv = conv + w_dw[tap][None, :] * widened[tap : tap + local_rows]
    activated = jax.nn.silu(bn_scale * conv + bn_shift).astype(jnp.bfloat16)
    result = attended + jnp.dot(activated, full_pw2, preferred_element_type=jnp.float32)
    return result.astype(jnp.bfloat16)


def swap(array, even, odd=None, groups=None):
    odd = even if odd is None else odd
    if groups is None:
        pairs = [(i, i ^ (odd if i & 1 else even)) for i in range(16)]
        return lax.ppermute(array, "frames", pairs)
    pairs = [(i, i ^ (odd if i & 1 else even)) for i in range(16 * groups)]
    return lax.ppermute(array, ("groups", "frames"), pairs)


def block_masks(order):
    masks = [0]
    for bit in order:
        masks = masks + [mask ^ bit for mask in masks]
    return masks


def source_of(me, j, even, odd, other_core):
    origin = me ^ 1 if other_core else me
    core = origin & 1
    return origin ^ jnp.where(core == 0, even[j], odd[j])


def prepare_kernel(
    scalars, feats_in, gain, w_qkv, w_out, w_pw1, w_pw2, normed, head0, head1, head2, head3, pack, feats, sems
):
    me, group = scalars[0], scalars[3]
    load = pltpu.make_async_copy(feats_in, feats, sems.at[0])
    load.start()
    att = w_qkv.shape[1] // 3
    width = feats.shape[1]
    copies = []
    for mask, out in zip(ALONG_Z, (head0, head1, head2, head3)):
        head = (me ^ mask) // 4
        for i in range(3):
            start = pl.multiple_of(i * att + head * HD, HD)
            copies.append((w_qkv.at[:, pl.ds(start, HD)], out.at[:, i * HD : (i + 1) * HD]))
    half = pack.shape[0]
    start = pl.multiple_of(group * half, half)
    copies.append((w_pw1.at[pl.ds(start, half)], pack.at[:, 0 : 2 * width]))
    copies.append((w_pw2.at[pl.ds(start, half)], pack.at[:, 2 * width : 3 * width]))
    side = pl.multiple_of(group * (width // 2), width // 2)
    copies.append((w_out.at[:, pl.ds(side, width // 2)], pack.at[:, 3 * width :]))
    copies = [pltpu.make_async_copy(a, b, sems.at[1 + i]) for i, (a, b) in enumerate(copies)]
    for copy in copies:
        copy.start()
    load.wait()
    values = feats[...].astype(jnp.float32)
    mean = jnp.mean(values, axis=-1, keepdims=True)
    centred = values - mean
    variance = jnp.mean(centred * centred, axis=-1, keepdims=True)
    normed[...] = (centred * lax.rsqrt(variance + EPSILON) * gain[...]).astype(jnp.bfloat16)
    for copy in copies:
        copy.wait()


def attention_kernel(
    scalars, xa, xb, xa_other, xb_other, own_w, other_w, *refs, rows, even, odd, w_masks, count
):
    outs, (x_all, w_all, keys, values, sems) = refs[:4], refs[4:]
    me, limit = scalars[0], scalars[1]
    depth = w_all.shape[0] // 16
    for other_core, (xs, ws) in enumerate((((xa, xb), own_w), ((xa_other, xb_other), other_w))):
        for j in range(8):
            src = source_of(me, j, w_masks, w_masks, other_core)
            pltpu.make_async_copy(
                ws.at[pl.ds(j * depth, depth)],
                w_all.at[pl.ds(pl.multiple_of(src * depth, depth), depth)],
                sems.at[0],
            ).start()
        for j in range(8):
            src = source_of(me, j, even, odd, other_core)
            pltpu.make_async_copy(
                xs[j // 4].at[pl.ds((j % 4) * rows, rows)],
                x_all.at[pl.ds(pl.multiple_of(EDGE + src * rows, EDGE), rows)],
                sems.at[1],
            ).start()
    width = x_all.shape[1]
    x_all[0:EDGE, :] = jnp.zeros((EDGE, width), jnp.bfloat16)
    x_all[EDGE + count : 2 * EDGE + count, :] = jnp.zeros((EDGE, width), jnp.bfloat16)
    pltpu.make_async_copy(w_all, w_all, sems.at[0]).wait()
    inner = x_all.at[pl.ds(EDGE, count)]
    pltpu.make_async_copy(inner, inner, sems.at[1]).wait()
    step = 512
    for r in range(count // step):
        both = jnp.dot(
            x_all[EDGE + r * step : EDGE + (r + 1) * step, :],
            w_all[:, HD:],
            preferred_element_type=jnp.float32,
        ).astype(jnp.bfloat16)
        keys[r * step : (r + 1) * step, :] = both[:, :HD]
        values[r * step : (r + 1) * step, :] = both[:, HD:]
    wide = rows + 2 * EDGE
    position = lax.broadcasted_iota(jnp.int32, (1, count), 1)
    valid = position < limit
    factor = LOG2E / math.sqrt(HD)
    for mask, out in zip(ALONG_Z, outs):
        start = pl.multiple_of((me ^ mask) * rows, EDGE)
        query = jnp.dot(
            x_all[pl.ds(start, wide), :], w_all[:, :HD], preferred_element_type=jnp.float32
        ).astype(jnp.bfloat16)
        scores = lax.dot_general(
            query, keys[...], (((1,), (1,)), ((), ())), preferred_element_type=jnp.float32
        )
        scores = jnp.where(valid, scores * factor, -1e30)
        weights = jnp.exp2(scores - jnp.max(scores, axis=-1, keepdims=True))
        totals = jnp.sum(weights, axis=-1, keepdims=True)
        summed = jnp.dot(
            weights.astype(jnp.bfloat16), values[...], preferred_element_type=jnp.float32
        )
        out[...] = (summed / totals).astype(jnp.bfloat16)


def bit_of(number, position):
    return (number >> position) & 1


def lane_sources(place, lanes, step):
    block = (lanes % (lanes.shape[1] // 2)) // step
    other = lanes // (lanes.shape[1] // 2)
    origin = place ^ other
    core = origin & 1
    for i, (even, odd) in enumerate(zip(PACK_EVEN, PACK_ODD)):
        origin = origin ^ (bit_of(block, i) * jnp.where(core == 0, even, odd))
    return origin


def tail_kernel(
    scalars, c0, c1, c2, c3, feats, gain, taps, bn_scale, bn_shift, pa, pb, pa_other, pb_other, out,
    v0, v1, v2, v3, wide_gated, sems, *, rows
):
    me, limit, place = scalars[0], scalars[1], scalars[2]
    held = (v0, v1, v2, v3)
    copies = [
        pltpu.make_async_copy(a, b, sems.at[i])
        for i, (a, b) in enumerate(zip((pa, pa_other, pb, pb_other), (v0, v2, v1, v3)))
    ]
    for copy in copies:
        copy.start()
    wide = rows + 2 * EDGE
    width = out.shape[1]
    quarter = width // 4
    step = v0.shape[0] // 8
    lanes = lax.broadcasted_iota(jnp.int32, (1, width), 1)
    source = lane_sources(place, lanes, step)
    index = (source & 15) * (2 * step) + (source // 16) * step + lanes % step
    line = lax.broadcasted_iota(jnp.int32, (width, width), 0)
    mixing = jnp.where(line == index, 1.0, 0.0).astype(jnp.bfloat16)

    def mixed(array, by):
        return jnp.dot(array, by, preferred_element_type=jnp.float32).astype(jnp.bfloat16)

    def times(array, start, stop):
        total = None
        for i, part in enumerate(held):
            term = jnp.dot(
                array[:, i * quarter : (i + 1) * quarter],
                part[:, start:stop],
                preferred_element_type=jnp.float32,
            )
            total = term if total is None else total + term
        return total

    row_out = (source & 15) * step + lanes % step
    side = source // 16
    heads = [((me ^ mask) // 4) for mask in ALONG_Z]
    halves = []
    spreads = [0.0, 0.0]
    small = lax.broadcasted_iota(jnp.int32, (HD, width), 0)
    for head, part in zip(heads, (c0, c1, c2, c3)):
        for h in range(2):
            by = jnp.where((small + head * HD == row_out) & (side == h), 1.0, 0.0).astype(jnp.bfloat16)
            spreads[h] = spreads[h] + jnp.dot(part[...], by, preferred_element_type=jnp.float32)
    for copy in copies:
        copy.wait()
    for h in range(2):
        halves.append(times(spreads[h].astype(jnp.bfloat16), 3 * width, 3 * width + width // 2))
    attended = feats[...].astype(jnp.float32) + jnp.concatenate(halves, axis=1)
    mean = jnp.mean(attended, axis=-1, keepdims=True)
    centred = attended - mean
    variance = jnp.mean(centred * centred, axis=-1, keepdims=True)
    normed2 = (centred * lax.rsqrt(variance + EPSILON) * gain[...]).astype(jnp.bfloat16)
    normed2 = mixed(normed2, mixing)
    value = times(normed2, 0, width)
    gate = times(normed2, width, 2 * width)
    frame = me * rows - EDGE + lax.broadcasted_iota(jnp.int32, (wide, 1), 0)
    inside = (frame >= 0) & (frame < limit)
    gated = jnp.where(inside, value * jax.nn.sigmoid(gate), 0.0)
    wide_gated[...] = gated.astype(jnp.bfloat16).astype(jnp.float32)
    half = (taps.shape[0] - 1) // 2
    conv = jnp.zeros((rows, out.shape[1]), jnp.float32)
    for tap in range(taps.shape[0]):
        at = EDGE - half + tap
        conv = conv + taps[tap : tap + 1, :] * wide_gated[at : at + rows, :]
    act = bn_scale[...] * conv + bn_shift[...]
    activated = (act * jax.nn.sigmoid(act)).astype(jnp.bfloat16)
    result = attended[EDGE : EDGE + rows, :] + times(mixed(activated, mixing), 2 * width, 3 * width)
    out[...] = result.astype(jnp.bfloat16)


def per_device(
    features, valid_length, ln1_gain, w_qkv, w_out, ln2_gain, w_pw1, w_dw, bn_scale, bn_shift, w_pw2
):
    rows, width = features.shape
    count = rows * 16
    depth = w_qkv.shape[0]
    me = lax.axis_index("frames")
    group = lax.axis_index("groups")
    groups = lax.axis_size("groups")
    scalars = jnp.stack([me, valid_length[0], 16 * group + me, group]).astype(jnp.int32)
    even, odd = block_masks(ORDER_EVEN), block_masks(ORDER_ODD)
    any_spec = pl.BlockSpec(memory_space=pl.ANY)
    hbm = pl.BlockSpec(memory_space=pltpu.HBM)
    smem = pl.BlockSpec(memory_space=pltpu.SMEM)
    vmem = pl.BlockSpec(memory_space=pltpu.VMEM)

    normed1, w_mine, w_8, w_4, w_12, pack = pl.pallas_call(
        prepare_kernel,
        name="prepare",
        out_shape=[jax.ShapeDtypeStruct((rows, width), jnp.bfloat16)]
        + [jax.ShapeDtypeStruct((depth, 3 * HD), jnp.bfloat16)] * 4
        + [jax.ShapeDtypeStruct((depth // 2, 3 * width + width // 2), jnp.bfloat16)],
        in_specs=[smem, hbm, vmem] + [hbm] * 4,
        out_specs=[vmem] * 6,
        scratch_shapes=[
            pltpu.VMEM((rows, width), jnp.bfloat16),
            pltpu.SemaphoreType.DMA((16,)),
        ],
        compiler_params=pltpu.CompilerParams(vmem_limit_bytes=60 << 20),
    )(scalars, features, ln1_gain.reshape(1, -1), w_qkv, w_out, w_pw1, w_pw2)

    def joined(*arrays):
        return lax.optimization_barrier(jnp.concatenate(arrays, axis=0))

    def pack_swap(held, stage):
        return swap(held, PACK_EVEN[stage], PACK_ODD[stage], groups)

    ahead = lax.ppermute(features[-EDGE:], "frames", [(i, i + 1) for i in range(15)])
    behind = lax.ppermute(features[:EDGE], "frames", [(i + 1, i) for i in range(15)])
    x1 = swap(normed1, ORDER_EVEN[0], ORDER_ODD[0])
    w_z = [swap(part, mask) for part, mask in zip((w_8, w_4, w_12), ALONG_Z[1:])]
    p2 = joined(pack, pack_swap(pack, 0))
    x2 = joined(normed1, x1)
    w4 = joined(w_mine, *w_z)
    w8 = joined(w4, swap(w4, 2))
    p2, w8, x2, ahead, behind = lax.optimization_barrier((p2, w8, x2, ahead, behind))

    p4 = joined(p2, pack_swap(p2, 1))
    xa = joined(x2, swap(x2, ORDER_EVEN[1], ORDER_ODD[1]))
    w_other = swap(w8, 1)
    xa, w_other = lax.optimization_barrier((xa, w_other))

    xb = swap(xa, ORDER_EVEN[2], ORDER_ODD[2])
    xa_other = swap(xa, 1)
    pa = joined(p4, pack_swap(p4, 2))
    xb, xa_other = lax.optimization_barrier((xb, xa_other))
    xb_other = swap(xb, 1)
    pb = pack_swap(pa, 3)
    pa_other = swap(pa, 1)

    wide = rows + 2 * EDGE
    w_masks = block_masks((8, 4, 2))
    contexts = pl.pallas_call(
        functools.partial(
            attention_kernel, rows=rows, even=even, odd=odd, w_masks=w_masks, count=count
        ),
        name="attention",
        out_shape=[jax.ShapeDtypeStruct((wide, HD), jnp.bfloat16)] * 4,
        in_specs=[smem] + [any_spec] * 6,
        out_specs=[vmem] * 4,
        scratch_shapes=[
            pltpu.VMEM((count + 2 * EDGE, width), jnp.bfloat16),
            pltpu.VMEM((16 * depth, 3 * HD), jnp.bfloat16),
            pltpu.VMEM((count, HD), jnp.bfloat16),
            pltpu.VMEM((count, HD), jnp.bfloat16),
            pltpu.SemaphoreType.DMA((2,)),
        ],
        compiler_params=pltpu.CompilerParams(vmem_limit_bytes=40 << 20),
        cost_estimate=pl.CostEstimate(
            flops=5_000_000_000, bytes_accessed=8 << 20, transcendentals=4 * wide * count
        ),
    )(scalars, xa, xb, xa_other, xb_other, w8, w_other)
    mine = [contexts[0]] + [swap(part, mask) for part, mask in zip(contexts[1:], ALONG_Z[1:])]
    pb, _ = lax.optimization_barrier((pb, mine))
    pb_other = swap(pb, 1)

    feats = jnp.concatenate([ahead, features, behind], axis=0)
    return pl.pallas_call(
        functools.partial(tail_kernel, rows=rows),
        name="tail",
        out_shape=jax.ShapeDtypeStruct((rows, width), jnp.bfloat16),
        in_specs=[smem] + [vmem] * 9 + [any_spec] * 4,
        out_specs=vmem,
        scratch_shapes=[
            pltpu.VMEM(pa.shape, jnp.bfloat16),
            pltpu.VMEM(pa.shape, jnp.bfloat16),
            pltpu.VMEM(pa.shape, jnp.bfloat16),
            pltpu.VMEM(pa.shape, jnp.bfloat16),
            pltpu.VMEM((wide, width), jnp.float32),
            pltpu.SemaphoreType.DMA((4,)),
        ],
        compiler_params=pltpu.CompilerParams(vmem_limit_bytes=40 << 20),
        cost_estimate=pl.CostEstimate(
            flops=1_200_000_000, bytes_accessed=8 << 20, transcendentals=wide * width * 2
        ),
    )(
        scalars,
        *mine,
        feats,
        ln2_gain.reshape(1, -1),
        w_dw,
        bn_scale.reshape(1, -1),
        bn_shift.reshape(1, -1),
        pa,
        pb,
        pa_other,
        pb_other,
    )


def solution(mesh):
    placed = (
        P(("groups", "frames"), None),
        P("groups"),
        P(),
        P("frames", None),
        P("frames", None),
        P(),
        P("frames", None),
        P(),
        P(),
        P(),
        P("frames", None),
    )
    return jax.shard_map(
        per_device if (mesh.shape["groups"], mesh.shape["frames"]) == (2, 16) else per_device_general,
        mesh=mesh,
        in_specs=placed,
        out_specs=P(("groups", "frames"), None),
        check_vma=False,
    )
```

```python
import functools
import math

import jax
import jax.numpy as jnp
from jax import lax
from jax.experimental import pallas as pl
from jax.experimental.pallas import tpu as pltpu
from jax.sharding import PartitionSpec as P

HEADS = 4
HD = 128

EPSILON = 1e-05
EDGE = 16
LOG2E = 1.4426950408889634

ORDER_EVEN = (8, 4, 2)
ORDER_ODD = (2, 8, 4)
PACK_EVEN = (8, 4, 2, 16)
PACK_ODD = (8, 2, 16, 4)
ALONG_Z = (0, 12, 4, 8)


def extended(cells, sides, width):
    for axis, dim in sides:
        count = lax.axis_size(axis)
        ends = count - 1
        head = lax.slice_in_dim(cells, 0, width, axis=dim)
        tail = lax.slice_in_dim(cells, cells.shape[dim] - width, cells.shape[dim], axis=dim)
        cells = jnp.concatenate(
            [
                lax.ppermute(tail, axis, [(i, (i + 1) % count) for i in range(ends)]),
                cells,
                lax.ppermute(head, axis, [((i + 1) % count, i) for i in range(ends)]),
            ],
            axis=dim,
        )
    return cells


def layer_norm(values, gain):
    values = values.astype(jnp.float32)
    mean = jnp.mean(values, axis=-1, keepdims=True)
    centred = values - mean
    variance = jnp.mean(centred * centred, axis=-1, keepdims=True)
    return (centred * lax.rsqrt(variance + EPSILON) * gain).astype(jnp.bfloat16)


def per_device_general(
    features, valid_length, ln1_gain, w_qkv, w_out, ln2_gain, w_pw1, w_dw, bn_scale, bn_shift, w_pw2
):
    limit = valid_length[0]
    local_rows = features.shape[0]
    width = features.shape[1]
    att_width = w_qkv.shape[1] // 3
    scale = 1.0 / math.sqrt(HD)
    full_out = lax.all_gather(w_out, "frames", axis=0, tiled=True)
    full_pw1 = lax.all_gather(w_pw1, "frames", axis=0, tiled=True)
    full_pw2 = lax.all_gather(w_pw2, "frames", axis=0, tiled=True)
    normed1 = layer_norm(features, ln1_gain)
    qkv = jnp.dot(
        normed1,
        lax.all_gather(w_qkv, "frames", axis=0, tiled=True),
        preferred_element_type=jnp.float32,
    ).astype(jnp.bfloat16)
    query_heads = qkv[:, :att_width].reshape(local_rows, HEADS, HD)
    pairs = lax.all_gather(qkv[:, att_width:], "frames", axis=0, tiled=True)
    count = pairs.shape[0]
    key_heads = pairs[:, :att_width].reshape(count, HEADS, HD)
    value_heads = pairs[:, att_width:].reshape(count, HEADS, HD)
    scores = (
        jnp.einsum("qhd,khd->hqk", query_heads, key_heads, preferred_element_type=jnp.float32)
        * scale
    )
    valid = (jnp.arange(count, dtype=jnp.int32) < limit)[None, None, :]
    scores = jnp.where(valid, scores, -1e30)
    maxima = jnp.max(scores, axis=-1)
    weights = jnp.where(valid, jnp.exp(scores - maxima[..., None]), 0.0)
    totals = jnp.sum(weights, axis=-1)
    summed = jnp.einsum(
        "hqk,khd->hqd",
        weights.astype(jnp.bfloat16),
        value_heads,
        preferred_element_type=jnp.float32,
    )
    context = (
        (summed / totals[..., None])
        .transpose(1, 0, 2)
        .reshape(local_rows, att_width)
        .astype(jnp.bfloat16)
    )
    attended = features.astype(jnp.float32) + jnp.dot(
        context, full_out, preferred_element_type=jnp.float32
    )
    normed2 = layer_norm(attended, ln2_gain)
    both = jnp.dot(normed2, full_pw1, preferred_element_type=jnp.float32)
    frame_index = lax.axis_index("frames") * local_rows + jnp.arange(local_rows, dtype=jnp.int32)
    frame_valid = (frame_index < limit)[:, None]
    gated = jnp.where(frame_valid, both[:, :width] * jax.nn.sigmoid(both[:, width:]), 0.0).astype(
        jnp.bfloat16
    )
    half_window = (w_dw.shape[0] - 1) // 2
    widened = extended(gated, (("frames", 0),), half_window).astype(jnp.float32)
    conv = jnp.zeros((local_rows, width), jnp.float32)
    for tap in range(w_dw.shape[0]):
        conv = conv + w_dw[tap][None, :] * widened[tap : tap + local_rows]
    activated = jax.nn.silu(bn_scale * conv + bn_shift).astype(jnp.bfloat16)
    result = attended + jnp.dot(activated, full_pw2, preferred_element_type=jnp.float32)
    return result.astype(jnp.bfloat16)


def swap(array, even, odd=None, groups=None):
    odd = even if odd is None else odd
    if groups is None:
        pairs = [(i, i ^ (odd if i & 1 else even)) for i in range(16)]
        return lax.ppermute(array, "frames", pairs)
    pairs = [(i, i ^ (odd if i & 1 else even)) for i in range(16 * groups)]
    return lax.ppermute(array, ("groups", "frames"), pairs)


def block_masks(order):
    masks = [0]
    for bit in order:
        masks = masks + [mask ^ bit for mask in masks]
    return masks


def source_of(me, j, even, odd, other_core):
    origin = me ^ 1 if other_core else me
    core = origin & 1
    return origin ^ jnp.where(core == 0, even[j], odd[j])


def prepare_kernel(
    scalars, feats_in, gain, w_qkv, w_out, w_pw1, w_pw2, normed, head0, head1, head2, head3, pack, feats, sems
):
    me, group = lax.axis_index("frames"), lax.axis_index("groups")
    load = pltpu.make_async_copy(feats_in, feats, sems.at[0])
    load.start()
    att = w_qkv.shape[1] // 3
    width = feats.shape[1]
    copies = []
    for mask, out in zip(ALONG_Z, (head0, head1, head2, head3)):
        head = (me ^ mask) // 4
        for i in range(3):
            start = pl.multiple_of(i * att + head * HD, HD)
            copies.append((w_qkv.at[:, pl.ds(start, HD)], out.at[:, i * HD : (i + 1) * HD]))
    half = pack.shape[0]
    start = pl.multiple_of(group * half, half)
    copies.append((w_pw1.at[pl.ds(start, half)], pack.at[:, 0 : 2 * width]))
    copies.append((w_pw2.at[pl.ds(start, half)], pack.at[:, 2 * width : 3 * width]))
    side = pl.multiple_of(group * (width // 2), width // 2)
    copies.append((w_out.at[:, pl.ds(side, width // 2)], pack.at[:, 3 * width :]))
    copies = [pltpu.make_async_copy(a, b, sems.at[1 + i]) for i, (a, b) in enumerate(copies)]
    for copy in copies:
        copy.start()
    load.wait()
    values = feats[...].astype(jnp.float32)
    mean = jnp.mean(values, axis=-1, keepdims=True)
    centred = values - mean
    variance = jnp.mean(centred * centred, axis=-1, keepdims=True)
    normed[...] = (centred * lax.rsqrt(variance + EPSILON) * gain[...]).astype(jnp.bfloat16)
    for copy in copies:
        copy.wait()


def attention_kernel(
    scalars, xa, xb, xa_other, xb_other, own_w, other_w, *refs, rows, even, odd, w_masks, count
):
    outs, (x_all, w_all, keys, values, sems) = refs[:4], refs[4:]
    me, limit = lax.axis_index("frames"), scalars[0]
    depth = w_all.shape[0] // 16
    for other_core, (xs, ws) in enumerate((((xa, xb), own_w), ((xa_other, xb_other), other_w))):
        for j in range(8):
            src = source_of(me, j, w_masks, w_masks, other_core)
            pltpu.make_async_copy(
                ws.at[pl.ds(j * depth, depth)],
                w_all.at[pl.ds(pl.multiple_of(src * depth, depth), depth)],
                sems.at[0],
            ).start()
        for j in range(8):
            src = source_of(me, j, even, odd, other_core)
            pltpu.make_async_copy(
                xs[j // 4].at[pl.ds((j % 4) * rows, rows)],
                x_all.at[pl.ds(pl.multiple_of(EDGE + src * rows, EDGE), rows)],
                sems.at[1],
            ).start()
    width = x_all.shape[1]
    x_all[0:EDGE, :] = jnp.zeros((EDGE, width), jnp.bfloat16)
    x_all[EDGE + count : 2 * EDGE + count, :] = jnp.zeros((EDGE, width), jnp.bfloat16)
    pltpu.make_async_copy(w_all, w_all, sems.at[0]).wait()
    inner = x_all.at[pl.ds(EDGE, count)]
    pltpu.make_async_copy(inner, inner, sems.at[1]).wait()
    step = 512
    for r in range(count // step):
        both = jnp.dot(
            x_all[EDGE + r * step : EDGE + (r + 1) * step, :],
            w_all[:, HD:],
            preferred_element_type=jnp.float32,
        ).astype(jnp.bfloat16)
        keys[r * step : (r + 1) * step, :] = both[:, :HD]
        values[r * step : (r + 1) * step, :] = both[:, HD:]
    wide = rows + 2 * EDGE
    position = lax.broadcasted_iota(jnp.int32, (1, count), 1)
    valid = position < limit
    factor = LOG2E / math.sqrt(HD)
    for mask, out in zip(ALONG_Z, outs):
        start = pl.multiple_of((me ^ mask) * rows, EDGE)
        query = jnp.dot(
            x_all[pl.ds(start, wide), :], w_all[:, :HD], preferred_element_type=jnp.float32
        ).astype(jnp.bfloat16)
        scores = lax.dot_general(
            query, keys[...], (((1,), (1,)), ((), ())), preferred_element_type=jnp.float32
        )
        scores = jnp.where(valid, scores * factor, -1e30)
        weights = jnp.exp2(scores - jnp.max(scores, axis=-1, keepdims=True))
        totals = jnp.sum(weights, axis=-1, keepdims=True)
        summed = jnp.dot(
            weights.astype(jnp.bfloat16), values[...], preferred_element_type=jnp.float32
        )
        out[...] = (summed / totals).astype(jnp.bfloat16)


def bit_of(number, position):
    return (number >> position) & 1


def lane_sources(place, lanes, step):
    block = (lanes % (lanes.shape[1] // 2)) // step
    other = lanes // (lanes.shape[1] // 2)
    origin = place ^ other
    core = origin & 1
    for i, (even, odd) in enumerate(zip(PACK_EVEN, PACK_ODD)):
        origin = origin ^ (bit_of(block, i) * jnp.where(core == 0, even, odd))
    return origin


def tail_kernel(
    scalars, c0, c1, c2, c3, feats, gain, taps, bn_scale, bn_shift, pa, pb, pa_other, pb_other, out,
    wide_gated, *, rows
):
    me, limit = lax.axis_index("frames"), scalars[0]
    place = lax.axis_index("groups") * 16 + me
    held = (pa, pb, pa_other, pb_other)
    wide = rows + 2 * EDGE
    width = out.shape[1]
    quarter = width // 4
    step = pa.shape[0] // 8
    lanes = lax.broadcasted_iota(jnp.int32, (1, width), 1)
    source = lane_sources(place, lanes, step)
    index = (source & 15) * (2 * step) + (source // 16) * step + lanes % step
    line = lax.broadcasted_iota(jnp.int32, (width, width), 0)
    mixing = jnp.where(line == index, 1.0, 0.0).astype(jnp.bfloat16)

    def mixed(array, by):
        return jnp.dot(array, by, preferred_element_type=jnp.float32).astype(jnp.bfloat16)

    def times(array, start, stop):
        total = None
        for i, part in enumerate(held):
            term = jnp.dot(
                array[:, i * quarter : (i + 1) * quarter],
                part[:, start:stop],
                preferred_element_type=jnp.float32,
            )
            total = term if total is None else total + term
        return total

    row_out = (source & 15) * step + lanes % step
    side = source // 16
    heads = [((me ^ mask) // 4) for mask in ALONG_Z]
    halves = []
    spreads = [0.0, 0.0]
    small = lax.broadcasted_iota(jnp.int32, (HD, width), 0)
    for head, part in zip(heads, (c0, c1, c2, c3)):
        for h in range(2):
            by = jnp.where((small + head * HD == row_out) & (side == h), 1.0, 0.0).astype(jnp.bfloat16)
            spreads[h] = spreads[h] + jnp.dot(part[...], by, preferred_element_type=jnp.float32)
    for h in range(2):
        halves.append(times(spreads[h].astype(jnp.bfloat16), 3 * width, 3 * width + width // 2))
    attended = feats[...].astype(jnp.float32) + jnp.concatenate(halves, axis=1)
    mean = jnp.mean(attended, axis=-1, keepdims=True)
    centred = attended - mean
    variance = jnp.mean(centred * centred, axis=-1, keepdims=True)
    normed2 = (centred * lax.rsqrt(variance + EPSILON) * gain[...]).astype(jnp.bfloat16)
    normed2 = mixed(normed2, mixing)
    value = times(normed2, 0, width)
    gate = times(normed2, width, 2 * width)
    frame = me * rows - EDGE + lax.broadcasted_iota(jnp.int32, (wide, 1), 0)
    inside = (frame >= 0) & (frame < limit)
    gated = jnp.where(inside, value * jax.nn.sigmoid(gate), 0.0)
    wide_gated[...] = gated.astype(jnp.bfloat16).astype(jnp.float32)
    half = (taps.shape[0] - 1) // 2
    conv = jnp.zeros((rows, out.shape[1]), jnp.float32)
    for tap in range(taps.shape[0]):
        at = EDGE - half + tap
        conv = conv + taps[tap : tap + 1, :] * wide_gated[at : at + rows, :]
    act = bn_scale[...] * conv + bn_shift[...]
    activated = (act * jax.nn.sigmoid(act)).astype(jnp.bfloat16)
    result = attended[EDGE : EDGE + rows, :] + times(mixed(activated, mixing), 2 * width, 3 * width)
    out[...] = result.astype(jnp.bfloat16)


def per_device(
    features, valid_length, ln1_gain, w_qkv, w_out, ln2_gain, w_pw1, w_dw, bn_scale, bn_shift, w_pw2
):
    rows, width = features.shape
    count = rows * 16
    depth = w_qkv.shape[0]
    groups = lax.axis_size("groups")
    scalars = valid_length
    even, odd = block_masks(ORDER_EVEN), block_masks(ORDER_ODD)
    any_spec = pl.BlockSpec(memory_space=pl.ANY)
    hbm = pl.BlockSpec(memory_space=pltpu.HBM)
    smem = pl.BlockSpec(memory_space=pltpu.SMEM)
    vmem = pl.BlockSpec(memory_space=pltpu.VMEM)

    normed1, w_mine, w_12, w_4, w_8, pack = pl.pallas_call(
        prepare_kernel,
        name="prepare",
        out_shape=[jax.ShapeDtypeStruct((rows, width), jnp.bfloat16)]
        + [jax.ShapeDtypeStruct((depth, 3 * HD), jnp.bfloat16)] * 4
        + [jax.ShapeDtypeStruct((depth // 2, 3 * width + width // 2), jnp.bfloat16)],
        in_specs=[smem, hbm, vmem] + [hbm] * 4,
        out_specs=[vmem] * 6,
        scratch_shapes=[
            pltpu.VMEM((rows, width), jnp.bfloat16),
            pltpu.SemaphoreType.DMA((16,)),
        ],
        compiler_params=pltpu.CompilerParams(vmem_limit_bytes=60 << 20),
    )(scalars, features, ln1_gain.reshape(1, -1), w_qkv, w_out, w_pw1, w_pw2)

    def joined(*arrays):
        return lax.optimization_barrier(jnp.concatenate(arrays, axis=0))

    def pack_swap(held, stage):
        return swap(held, PACK_EVEN[stage], PACK_ODD[stage], groups)

    ahead = lax.ppermute(features[-EDGE:], "frames", [(i, i + 1) for i in range(15)])
    behind = lax.ppermute(features[:EDGE], "frames", [(i + 1, i) for i in range(15)])
    x1 = swap(normed1, ORDER_EVEN[0], ORDER_ODD[0])
    w_z = [swap(part, mask) for part, mask in zip((w_12, w_4, w_8), ALONG_Z[1:])]
    p2 = joined(pack, pack_swap(pack, 0))
    x2 = joined(normed1, x1)
    w4 = joined(w_mine, *w_z)
    w8 = joined(w4, swap(w4, 2))
    p2, w8, x2, ahead, behind = lax.optimization_barrier((p2, w8, x2, ahead, behind))

    p4 = joined(p2, pack_swap(p2, 1))
    xa = joined(x2, swap(x2, ORDER_EVEN[1], ORDER_ODD[1]))
    w_other = swap(w8, 1)
    xa, w_other = lax.optimization_barrier((xa, w_other))

    xb = swap(xa, ORDER_EVEN[2], ORDER_ODD[2])
    xa_other = swap(xa, 1)
    pa = joined(p4, pack_swap(p4, 2))
    xb, xa_other = lax.optimization_barrier((xb, xa_other))
    xb_other = swap(xb, 1)
    pb = pack_swap(pa, 3)
    pa_other = swap(pa, 1)

    wide = rows + 2 * EDGE
    w_masks = list(ALONG_Z) + [mask ^ 2 for mask in ALONG_Z]
    contexts = pl.pallas_call(
        functools.partial(
            attention_kernel, rows=rows, even=even, odd=odd, w_masks=w_masks, count=count
        ),
        name="attention",
        out_shape=[jax.ShapeDtypeStruct((wide, HD), jnp.bfloat16)] * 4,
        in_specs=[smem] + [any_spec] * 6,
        out_specs=[vmem] * 4,
        scratch_shapes=[
            pltpu.VMEM((count + 2 * EDGE, width), jnp.bfloat16),
            pltpu.VMEM((16 * depth, 3 * HD), jnp.bfloat16),
            pltpu.VMEM((count, HD), jnp.bfloat16),
            pltpu.VMEM((count, HD), jnp.bfloat16),
            pltpu.SemaphoreType.DMA((2,)),
        ],
        compiler_params=pltpu.CompilerParams(vmem_limit_bytes=40 << 20),
        cost_estimate=pl.CostEstimate(
            flops=5_000_000_000, bytes_accessed=8 << 20, transcendentals=4 * wide * count
        ),
    )(scalars, xa, xb, xa_other, xb_other, w8, w_other)
    mine = [contexts[0]] + [swap(part, mask) for part, mask in zip(contexts[1:], ALONG_Z[1:])]
    pb, _ = lax.optimization_barrier((pb, mine))
    pb_other = swap(pb, 1)

    feats = jnp.concatenate([ahead, features, behind], axis=0)
    return pl.pallas_call(
        functools.partial(tail_kernel, rows=rows),
        name="tail",
        out_shape=jax.ShapeDtypeStruct((rows, width), jnp.bfloat16),
        in_specs=[smem] + [vmem] * 13,
        out_specs=vmem,
        scratch_shapes=[
            pltpu.VMEM((wide, width), jnp.float32),
        ],
        compiler_params=pltpu.CompilerParams(vmem_limit_bytes=40 << 20),
        cost_estimate=pl.CostEstimate(
            flops=1_200_000_000, bytes_accessed=8 << 20, transcendentals=wide * width * 2
        ),
    )(
        scalars,
        *mine,
        feats,
        ln2_gain.reshape(1, -1),
        w_dw,
        bn_scale.reshape(1, -1),
        bn_shift.reshape(1, -1),
        pa,
        pb,
        pa_other,
        pb_other,
    )


def solution(mesh):
    placed = (
        P(("groups", "frames"), None),
        P("groups"),
        P(),
        P("frames", None),
        P("frames", None),
        P(),
        P("frames", None),
        P(),
        P(),
        P(),
        P("frames", None),
    )
    return jax.shard_map(
        per_device if (mesh.shape["groups"], mesh.shape["frames"]) == (2, 16) else per_device_general,
        mesh=mesh,
        in_specs=placed,
        out_specs=P(("groups", "frames"), None),
        check_vma=False,
    )
```

```python
import functools
import math

import jax
import jax.numpy as jnp
from jax import lax
from jax.experimental import pallas as pl
from jax.experimental.pallas import tpu as pltpu
from jax.sharding import PartitionSpec as P

HEADS = 4
HD = 128

EPSILON = 1e-05
EDGE = 16
LOG2E = 1.4426950408889634

ORDER_EVEN = (8, 4, 2)
ORDER_ODD = (2, 8, 4)
PACK_EVEN = (8, 2, 16, 4)
PACK_ODD = (8, 4, 16, 2)
ALONG_Z = (0, 12, 4, 8)


def extended(cells, sides, width):
    for axis, dim in sides:
        count = lax.axis_size(axis)
        ends = count - 1
        head = lax.slice_in_dim(cells, 0, width, axis=dim)
        tail = lax.slice_in_dim(cells, cells.shape[dim] - width, cells.shape[dim], axis=dim)
        cells = jnp.concatenate(
            [
                lax.ppermute(tail, axis, [(i, (i + 1) % count) for i in range(ends)]),
                cells,
                lax.ppermute(head, axis, [((i + 1) % count, i) for i in range(ends)]),
            ],
            axis=dim,
        )
    return cells


def layer_norm(values, gain):
    values = values.astype(jnp.float32)
    mean = jnp.mean(values, axis=-1, keepdims=True)
    centred = values - mean
    variance = jnp.mean(centred * centred, axis=-1, keepdims=True)
    return (centred * lax.rsqrt(variance + EPSILON) * gain).astype(jnp.bfloat16)


def per_device_general(
    features, valid_length, ln1_gain, w_qkv, w_out, ln2_gain, w_pw1, w_dw, bn_scale, bn_shift, w_pw2
):
    limit = valid_length[0]
    local_rows = features.shape[0]
    width = features.shape[1]
    att_width = w_qkv.shape[1] // 3
    scale = 1.0 / math.sqrt(HD)
    full_out = lax.all_gather(w_out, "frames", axis=0, tiled=True)
    full_pw1 = lax.all_gather(w_pw1, "frames", axis=0, tiled=True)
    full_pw2 = lax.all_gather(w_pw2, "frames", axis=0, tiled=True)
    normed1 = layer_norm(features, ln1_gain)
    qkv = jnp.dot(
        normed1,
        lax.all_gather(w_qkv, "frames", axis=0, tiled=True),
        preferred_element_type=jnp.float32,
    ).astype(jnp.bfloat16)
    query_heads = qkv[:, :att_width].reshape(local_rows, HEADS, HD)
    pairs = lax.all_gather(qkv[:, att_width:], "frames", axis=0, tiled=True)
    count = pairs.shape[0]
    key_heads = pairs[:, :att_width].reshape(count, HEADS, HD)
    value_heads = pairs[:, att_width:].reshape(count, HEADS, HD)
    scores = (
        jnp.einsum("qhd,khd->hqk", query_heads, key_heads, preferred_element_type=jnp.float32)
        * scale
    )
    valid = (jnp.arange(count, dtype=jnp.int32) < limit)[None, None, :]
    scores = jnp.where(valid, scores, -1e30)
    maxima = jnp.max(scores, axis=-1)
    weights = jnp.where(valid, jnp.exp(scores - maxima[..., None]), 0.0)
    totals = jnp.sum(weights, axis=-1)
    summed = jnp.einsum(
        "hqk,khd->hqd",
        weights.astype(jnp.bfloat16),
        value_heads,
        preferred_element_type=jnp.float32,
    )
    context = (
        (summed / totals[..., None])
        .transpose(1, 0, 2)
        .reshape(local_rows, att_width)
        .astype(jnp.bfloat16)
    )
    attended = features.astype(jnp.float32) + jnp.dot(
        context, full_out, preferred_element_type=jnp.float32
    )
    normed2 = layer_norm(attended, ln2_gain)
    both = jnp.dot(normed2, full_pw1, preferred_element_type=jnp.float32)
    frame_index = lax.axis_index("frames") * local_rows + jnp.arange(local_rows, dtype=jnp.int32)
    frame_valid = (frame_index < limit)[:, None]
    gated = jnp.where(frame_valid, both[:, :width] * jax.nn.sigmoid(both[:, width:]), 0.0).astype(
        jnp.bfloat16
    )
    half_window = (w_dw.shape[0] - 1) // 2
    widened = extended(gated, (("frames", 0),), half_window).astype(jnp.float32)
    conv = jnp.zeros((local_rows, width), jnp.float32)
    for tap in range(w_dw.shape[0]):
        conv = conv + w_dw[tap][None, :] * widened[tap : tap + local_rows]
    activated = jax.nn.silu(bn_scale * conv + bn_shift).astype(jnp.bfloat16)
    result = attended + jnp.dot(activated, full_pw2, preferred_element_type=jnp.float32)
    return result.astype(jnp.bfloat16)


def swap(array, even, odd=None, groups=None):
    odd = even if odd is None else odd
    if groups is None:
        pairs = [(i, i ^ (odd if i & 1 else even)) for i in range(16)]
        return lax.ppermute(array, "frames", pairs)
    pairs = [(i, i ^ (odd if i & 1 else even)) for i in range(16 * groups)]
    return lax.ppermute(array, ("groups", "frames"), pairs)


def block_masks(order):
    masks = [0]
    for bit in order:
        masks = masks + [mask ^ bit for mask in masks]
    return masks


def source_of(me, j, even, odd, other_core):
    origin = me ^ 1 if other_core else me
    core = origin & 1
    return origin ^ jnp.where(core == 0, even[j], odd[j])


def prepare_kernel(
    scalars, feats_in, gain, w_qkv, w_out, w_pw1, w_pw2, normed, head0, head1, head2, head3, pack, feats, sems
):
    me, group = lax.axis_index("frames"), lax.axis_index("groups")
    load = pltpu.make_async_copy(feats_in, feats, sems.at[0])
    load.start()
    att = w_qkv.shape[1] // 3
    width = feats.shape[1]
    copies = []
    for mask, out in zip(ALONG_Z, (head0, head1, head2, head3)):
        head = (me ^ mask) // 4
        for i in range(3):
            start = pl.multiple_of(i * att + head * HD, HD)
            copies.append((w_qkv.at[:, pl.ds(start, HD)], out.at[:, i * HD : (i + 1) * HD]))
    half = pack.shape[0]
    start = pl.multiple_of(group * half, half)
    copies.append((w_pw1.at[pl.ds(start, half)], pack.at[:, 0 : 2 * width]))
    copies.append((w_pw2.at[pl.ds(start, half)], pack.at[:, 2 * width : 3 * width]))
    side = pl.multiple_of(group * (width // 2), width // 2)
    copies.append((w_out.at[:, pl.ds(side, width // 2)], pack.at[:, 3 * width :]))
    copies = [pltpu.make_async_copy(a, b, sems.at[1 + i]) for i, (a, b) in enumerate(copies)]
    for copy in copies:
        copy.start()
    load.wait()
    values = feats[...].astype(jnp.float32)
    mean = jnp.mean(values, axis=-1, keepdims=True)
    centred = values - mean
    variance = jnp.mean(centred * centred, axis=-1, keepdims=True)
    normed[...] = (centred * lax.rsqrt(variance + EPSILON) * gain[...]).astype(jnp.bfloat16)
    for copy in copies:
        copy.wait()


def attention_kernel(
    scalars, xa, xb, xa_other, xb_other, own_w, other_w, *refs, rows, even, odd, w_masks, count
):
    outs, (x_all, w_all, keys, values) = refs[:4], refs[4:]
    me, limit = lax.axis_index("frames"), scalars[0]
    depth = w_all.shape[0] // 16
    width = x_all.shape[1]
    x_all[0:EDGE, :] = jnp.zeros((EDGE, width), jnp.bfloat16)
    x_all[EDGE + count : 2 * EDGE + count, :] = jnp.zeros((EDGE, width), jnp.bfloat16)
    for other_core, ws in enumerate((own_w, other_w)):
        for j in range(8):
            src = source_of(me, j, w_masks, w_masks, other_core)
            row = pl.multiple_of(src * depth, depth)
            w_all[pl.ds(row, depth), :] = ws[j * depth : (j + 1) * depth, :]
    for part, xs in enumerate((xa, xb, xa_other, xb_other)):
        both = jnp.dot(
            xs[...], w_all[:, HD:], preferred_element_type=jnp.float32
        ).astype(jnp.bfloat16)
        for i in range(4):
            src = source_of(me, 4 * (part % 2) + i, even, odd, part // 2)
            row = pl.multiple_of(src * rows, rows)
            here = slice(i * rows, (i + 1) * rows)
            keys[pl.ds(row, rows), :] = both[here, :HD]
            values[pl.ds(row, rows), :] = both[here, HD:]
            x_all[pl.ds(pl.multiple_of(row + EDGE, EDGE), rows), :] = xs[here, :]
    wide = rows + 2 * EDGE
    position = lax.broadcasted_iota(jnp.int32, (1, count), 1)
    valid = position < limit
    factor = LOG2E / math.sqrt(HD)
    for mask, out in zip(ALONG_Z, outs):
        start = pl.multiple_of((me ^ mask) * rows, EDGE)
        query = jnp.dot(
            x_all[pl.ds(start, wide), :], w_all[:, :HD], preferred_element_type=jnp.float32
        ).astype(jnp.bfloat16)
        scores = lax.dot_general(
            query, keys[...], (((1,), (1,)), ((), ())), preferred_element_type=jnp.float32
        )
        scores = jnp.where(valid, scores * factor, -1e30)
        weights = jnp.exp2(scores - jnp.max(scores, axis=-1, keepdims=True))
        totals = jnp.sum(weights, axis=-1, keepdims=True)
        summed = jnp.dot(
            weights.astype(jnp.bfloat16), values[...], preferred_element_type=jnp.float32
        )
        out[...] = (summed / totals).astype(jnp.bfloat16)


def bit_of(number, position):
    return (number >> position) & 1


def lane_sources(place, lanes, step):
    block = (lanes % (lanes.shape[1] // 2)) // step
    other = lanes // (lanes.shape[1] // 2)
    origin = place ^ other
    core = origin & 1
    for i, (even, odd) in enumerate(zip(PACK_EVEN, PACK_ODD)):
        origin = origin ^ (bit_of(block, i) * jnp.where(core == 0, even, odd))
    return origin


def tail_kernel(
    scalars, c0, c1, c2, c3, feats, gain, taps, bn_scale, bn_shift, pa, pb, pa_other, pb_other, out,
    wide_gated, *, rows
):
    me, limit = lax.axis_index("frames"), scalars[0]
    place = lax.axis_index("groups") * 16 + me
    held = (pa, pb, pa_other, pb_other)
    wide = rows + 2 * EDGE
    width = out.shape[1]
    quarter = width // 4
    step = pa.shape[0] // 8
    lanes = lax.broadcasted_iota(jnp.int32, (1, width), 1)
    source = lane_sources(place, lanes, step)
    index = (source & 15) * (2 * step) + (source // 16) * step + lanes % step
    line = lax.broadcasted_iota(jnp.int32, (width, width), 0)
    mixing = jnp.where(line == index, 1.0, 0.0).astype(jnp.bfloat16)

    def mixed(array, by):
        return jnp.dot(array, by, preferred_element_type=jnp.float32).astype(jnp.bfloat16)

    def times(array, start, stop):
        total = None
        for i, part in enumerate(held):
            term = jnp.dot(
                array[:, i * quarter : (i + 1) * quarter],
                part[:, start:stop],
                preferred_element_type=jnp.float32,
            )
            total = term if total is None else total + term
        return total

    row_out = (source & 15) * step + lanes % step
    side = source // 16
    heads = [((me ^ mask) // 4) for mask in ALONG_Z]
    halves = []
    spreads = [0.0, 0.0]
    small = lax.broadcasted_iota(jnp.int32, (HD, width), 0)
    for head, part in zip(heads, (c0, c1, c2, c3)):
        for h in range(2):
            by = jnp.where((small + head * HD == row_out) & (side == h), 1.0, 0.0).astype(jnp.bfloat16)
            spreads[h] = spreads[h] + jnp.dot(part[...], by, preferred_element_type=jnp.float32)
    for h in range(2):
        halves.append(times(spreads[h].astype(jnp.bfloat16), 3 * width, 3 * width + width // 2))
    attended = feats[...].astype(jnp.float32) + jnp.concatenate(halves, axis=1)
    mean = jnp.mean(attended, axis=-1, keepdims=True)
    centred = attended - mean
    variance = jnp.mean(centred * centred, axis=-1, keepdims=True)
    normed2 = (centred * lax.rsqrt(variance + EPSILON) * gain[...]).astype(jnp.bfloat16)
    normed2 = mixed(normed2, mixing)
    value = times(normed2, 0, width)
    gate = times(normed2, width, 2 * width)
    frame = me * rows - EDGE + lax.broadcasted_iota(jnp.int32, (wide, 1), 0)
    inside = (frame >= 0) & (frame < limit)
    gated = jnp.where(inside, value * jax.nn.sigmoid(gate), 0.0)
    wide_gated[...] = gated.astype(jnp.bfloat16).astype(jnp.float32)
    half = (taps.shape[0] - 1) // 2
    conv = jnp.zeros((rows, out.shape[1]), jnp.float32)
    for tap in range(taps.shape[0]):
        at = EDGE - half + tap
        conv = conv + taps[tap : tap + 1, :] * wide_gated[at : at + rows, :]
    act = bn_scale[...] * conv + bn_shift[...]
    activated = (act * jax.nn.sigmoid(act)).astype(jnp.bfloat16)
    result = attended[EDGE : EDGE + rows, :] + times(mixed(activated, mixing), 2 * width, 3 * width)
    out[...] = result.astype(jnp.bfloat16)


def per_device(
    features, valid_length, ln1_gain, w_qkv, w_out, ln2_gain, w_pw1, w_dw, bn_scale, bn_shift, w_pw2
):
    rows, width = features.shape
    count = rows * 16
    depth = w_qkv.shape[0]
    groups = lax.axis_size("groups")
    scalars = valid_length
    even, odd = block_masks(ORDER_EVEN), block_masks(ORDER_ODD)
    hbm = pl.BlockSpec(memory_space=pltpu.HBM)
    smem = pl.BlockSpec(memory_space=pltpu.SMEM)
    vmem = pl.BlockSpec(memory_space=pltpu.VMEM)

    normed1, w_mine, w_12, w_4, w_8, pack = pl.pallas_call(
        prepare_kernel,
        name="prepare",
        out_shape=[jax.ShapeDtypeStruct((rows, width), jnp.bfloat16)]
        + [jax.ShapeDtypeStruct((depth, 3 * HD), jnp.bfloat16)] * 4
        + [jax.ShapeDtypeStruct((depth // 2, 3 * width + width // 2), jnp.bfloat16)],
        in_specs=[smem, hbm, vmem] + [hbm] * 4,
        out_specs=[vmem] * 6,
        scratch_shapes=[
            pltpu.VMEM((rows, width), jnp.bfloat16),
            pltpu.SemaphoreType.DMA((16,)),
        ],
        compiler_params=pltpu.CompilerParams(vmem_limit_bytes=60 << 20),
    )(scalars, features, ln1_gain.reshape(1, -1), w_qkv, w_out, w_pw1, w_pw2)

    def joined(*arrays):
        return lax.optimization_barrier(jnp.concatenate(arrays, axis=0))

    def pack_swap(held, stage):
        return swap(held, PACK_EVEN[stage], PACK_ODD[stage], groups)

    ahead = lax.ppermute(features[-EDGE:], "frames", [(i, i + 1) for i in range(15)])
    behind = lax.ppermute(features[:EDGE], "frames", [(i + 1, i) for i in range(15)])
    x1 = swap(normed1, ORDER_EVEN[0], ORDER_ODD[0])
    w_z = [swap(part, mask) for part, mask in zip((w_12, w_4, w_8), ALONG_Z[1:])]
    p2 = joined(pack, pack_swap(pack, 0))
    x2 = joined(normed1, x1)
    w4 = joined(w_mine, *w_z)
    w8 = joined(w4, swap(w4, 2))
    p2, w8, x2, ahead, behind = lax.optimization_barrier((p2, w8, x2, ahead, behind))

    p4 = joined(p2, pack_swap(p2, 1))
    xa = joined(x2, swap(x2, ORDER_EVEN[1], ORDER_ODD[1]))
    w_other = swap(w8, 1)
    xa, w_other = lax.optimization_barrier((xa, w_other))

    xb = swap(xa, ORDER_EVEN[2], ORDER_ODD[2])
    xa_other = swap(xa, 1)
    pa = joined(p4, pack_swap(p4, 2))
    xb_other = swap(xb, 1)
    pb = pack_swap(pa, 3)
    pa_other = swap(pa, 1)

    wide = rows + 2 * EDGE
    w_masks = list(ALONG_Z) + [mask ^ 2 for mask in ALONG_Z]
    contexts = pl.pallas_call(
        functools.partial(
            attention_kernel, rows=rows, even=even, odd=odd, w_masks=w_masks, count=count
        ),
        name="attention",
        out_shape=[jax.ShapeDtypeStruct((wide, HD), jnp.bfloat16)] * 4,
        in_specs=[smem] + [vmem] * 6,
        out_specs=[vmem] * 4,
        scratch_shapes=[
            pltpu.VMEM((count + 2 * EDGE, width), jnp.bfloat16),
            pltpu.VMEM((16 * depth, 3 * HD), jnp.bfloat16),
            pltpu.VMEM((count, HD), jnp.bfloat16),
            pltpu.VMEM((count, HD), jnp.bfloat16),
        ],
        compiler_params=pltpu.CompilerParams(vmem_limit_bytes=40 << 20),
        cost_estimate=pl.CostEstimate(
            flops=5_000_000_000, bytes_accessed=8 << 20, transcendentals=4 * wide * count
        ),
    )(scalars, xa, xb, xa_other, xb_other, w8, w_other)
    mine = [contexts[0]] + [swap(part, mask) for part, mask in zip(contexts[1:], ALONG_Z[1:])]
    pb, _ = lax.optimization_barrier((pb, mine))
    pb_other = swap(pb, 1)

    feats = jnp.concatenate([ahead, features, behind], axis=0)
    return pl.pallas_call(
        functools.partial(tail_kernel, rows=rows),
        name="tail",
        out_shape=jax.ShapeDtypeStruct((rows, width), jnp.bfloat16),
        in_specs=[smem] + [vmem] * 13,
        out_specs=vmem,
        scratch_shapes=[
            pltpu.VMEM((wide, width), jnp.float32),
        ],
        compiler_params=pltpu.CompilerParams(vmem_limit_bytes=40 << 20),
        cost_estimate=pl.CostEstimate(
            flops=1_200_000_000, bytes_accessed=8 << 20, transcendentals=wide * width * 2
        ),
    )(
        scalars,
        *mine,
        feats,
        ln2_gain.reshape(1, -1),
        w_dw,
        bn_scale.reshape(1, -1),
        bn_shift.reshape(1, -1),
        pa,
        pb,
        pa_other,
        pb_other,
    )


def solution(mesh):
    placed = (
        P(("groups", "frames"), None),
        P("groups"),
        P(),
        P("frames", None),
        P("frames", None),
        P(),
        P("frames", None),
        P(),
        P(),
        P(),
        P("frames", None),
    )
    return jax.shard_map(
        per_device if (mesh.shape["groups"], mesh.shape["frames"]) == (2, 16) else per_device_general,
        mesh=mesh,
        in_specs=placed,
        out_specs=P(("groups", "frames"), None),
        check_vma=False,
    )
```

```python
import functools
import math

import jax
import jax.numpy as jnp
from jax import lax
from jax.experimental import pallas as pl
from jax.experimental.pallas import tpu as pltpu
from jax.sharding import PartitionSpec as P

HEADS = 4
HD = 128

EPSILON = 1e-05
EDGE = 16
LOG2E = 1.4426950408889634

ORDER_EVEN = (8, 4, 2)
ORDER_ODD = (2, 8, 4)
PACK_EVEN = (8, 2, 16, 4)
PACK_ODD = (8, 4, 16, 2)
ALONG_Z = (0, 12, 4, 8)


def extended(cells, sides, width):
    for axis, dim in sides:
        count = lax.axis_size(axis)
        ends = count - 1
        head = lax.slice_in_dim(cells, 0, width, axis=dim)
        tail = lax.slice_in_dim(cells, cells.shape[dim] - width, cells.shape[dim], axis=dim)
        cells = jnp.concatenate(
            [
                lax.ppermute(tail, axis, [(i, (i + 1) % count) for i in range(ends)]),
                cells,
                lax.ppermute(head, axis, [((i + 1) % count, i) for i in range(ends)]),
            ],
            axis=dim,
        )
    return cells


def layer_norm(values, gain):
    values = values.astype(jnp.float32)
    mean = jnp.mean(values, axis=-1, keepdims=True)
    centred = values - mean
    variance = jnp.mean(centred * centred, axis=-1, keepdims=True)
    return (centred * lax.rsqrt(variance + EPSILON) * gain).astype(jnp.bfloat16)


def per_device_general(
    features, valid_length, ln1_gain, w_qkv, w_out, ln2_gain, w_pw1, w_dw, bn_scale, bn_shift, w_pw2
):
    limit = valid_length[0]
    local_rows = features.shape[0]
    width = features.shape[1]
    att_width = w_qkv.shape[1] // 3
    scale = 1.0 / math.sqrt(HD)
    full_out = lax.all_gather(w_out, "frames", axis=0, tiled=True)
    full_pw1 = lax.all_gather(w_pw1, "frames", axis=0, tiled=True)
    full_pw2 = lax.all_gather(w_pw2, "frames", axis=0, tiled=True)
    normed1 = layer_norm(features, ln1_gain)
    qkv = jnp.dot(
        normed1,
        lax.all_gather(w_qkv, "frames", axis=0, tiled=True),
        preferred_element_type=jnp.float32,
    ).astype(jnp.bfloat16)
    query_heads = qkv[:, :att_width].reshape(local_rows, HEADS, HD)
    pairs = lax.all_gather(qkv[:, att_width:], "frames", axis=0, tiled=True)
    count = pairs.shape[0]
    key_heads = pairs[:, :att_width].reshape(count, HEADS, HD)
    value_heads = pairs[:, att_width:].reshape(count, HEADS, HD)
    scores = (
        jnp.einsum("qhd,khd->hqk", query_heads, key_heads, preferred_element_type=jnp.float32)
        * scale
    )
    valid = (jnp.arange(count, dtype=jnp.int32) < limit)[None, None, :]
    scores = jnp.where(valid, scores, -1e30)
    maxima = jnp.max(scores, axis=-1)
    weights = jnp.where(valid, jnp.exp(scores - maxima[..., None]), 0.0)
    totals = jnp.sum(weights, axis=-1)
    summed = jnp.einsum(
        "hqk,khd->hqd",
        weights.astype(jnp.bfloat16),
        value_heads,
        preferred_element_type=jnp.float32,
    )
    context = (
        (summed / totals[..., None])
        .transpose(1, 0, 2)
        .reshape(local_rows, att_width)
        .astype(jnp.bfloat16)
    )
    attended = features.astype(jnp.float32) + jnp.dot(
        context, full_out, preferred_element_type=jnp.float32
    )
    normed2 = layer_norm(attended, ln2_gain)
    both = jnp.dot(normed2, full_pw1, preferred_element_type=jnp.float32)
    frame_index = lax.axis_index("frames") * local_rows + jnp.arange(local_rows, dtype=jnp.int32)
    frame_valid = (frame_index < limit)[:, None]
    gated = jnp.where(frame_valid, both[:, :width] * jax.nn.sigmoid(both[:, width:]), 0.0).astype(
        jnp.bfloat16
    )
    half_window = (w_dw.shape[0] - 1) // 2
    widened = extended(gated, (("frames", 0),), half_window).astype(jnp.float32)
    conv = jnp.zeros((local_rows, width), jnp.float32)
    for tap in range(w_dw.shape[0]):
        conv = conv + w_dw[tap][None, :] * widened[tap : tap + local_rows]
    activated = jax.nn.silu(bn_scale * conv + bn_shift).astype(jnp.bfloat16)
    result = attended + jnp.dot(activated, full_pw2, preferred_element_type=jnp.float32)
    return result.astype(jnp.bfloat16)


def swap(array, even, odd=None, groups=None):
    odd = even if odd is None else odd
    if groups is None:
        pairs = [(i, i ^ (odd if i & 1 else even)) for i in range(16)]
        return lax.ppermute(array, "frames", pairs)
    pairs = [(i, i ^ (odd if i & 1 else even)) for i in range(16 * groups)]
    return lax.ppermute(array, ("groups", "frames"), pairs)


def block_masks(order):
    masks = [0]
    for bit in order:
        masks = masks + [mask ^ bit for mask in masks]
    return masks


def source_of(me, j, even, odd, other_core):
    origin = me ^ 1 if other_core else me
    core = origin & 1
    return origin ^ jnp.where(core == 0, even[j], odd[j])


def prepare_kernel(
    scalars, feats_in, gain, w_qkv, w_out, w_pw1, w_pw2, normed, head0, head1, head2, head3, pack, feats, sems
):
    me, group = lax.axis_index("frames"), lax.axis_index("groups")
    load = pltpu.make_async_copy(feats_in, feats, sems.at[0])
    load.start()
    att = w_qkv.shape[1] // 3
    width = feats.shape[1]
    copies = []
    for mask, out in zip(ALONG_Z, (head0, head1, head2, head3)):
        head = (me ^ mask) // 4
        for i in range(3):
            start = pl.multiple_of(i * att + head * HD, HD)
            copies.append((w_qkv.at[:, pl.ds(start, HD)], out.at[:, i * HD : (i + 1) * HD]))
    half = pack.shape[0]
    start = pl.multiple_of(group * half, half)
    copies.append((w_pw1.at[pl.ds(start, half)], pack.at[:, 0 : 2 * width]))
    copies.append((w_pw2.at[pl.ds(start, half)], pack.at[:, 2 * width : 3 * width]))
    side = pl.multiple_of(group * (width // 2), width // 2)
    copies.append((w_out.at[:, pl.ds(side, width // 2)], pack.at[:, 3 * width :]))
    copies = [pltpu.make_async_copy(a, b, sems.at[1 + i]) for i, (a, b) in enumerate(copies)]
    for copy in copies:
        copy.start()
    load.wait()
    values = feats[...].astype(jnp.float32)
    mean = jnp.mean(values, axis=-1, keepdims=True)
    centred = values - mean
    variance = jnp.mean(centred * centred, axis=-1, keepdims=True)
    normed[...] = (centred * lax.rsqrt(variance + EPSILON) * gain[...]).astype(jnp.bfloat16)
    for copy in copies:
        copy.wait()


def attention_kernel(
    scalars, xa, xb, xa_other, xb_other, own_w, other_w, *refs, rows, even, odd, w_masks, count
):
    outs, (x_all, w_all, keys, values) = refs[:4], refs[4:]
    me, limit = lax.axis_index("frames"), scalars[0]
    depth = w_all.shape[0] // 16
    width = x_all.shape[1]
    x_all[0:EDGE, :] = jnp.zeros((EDGE, width), jnp.bfloat16)
    x_all[EDGE + count : 2 * EDGE + count, :] = jnp.zeros((EDGE, width), jnp.bfloat16)
    for other_core, ws in enumerate((own_w, other_w)):
        for j in range(8):
            src = source_of(me, j, w_masks, w_masks, other_core)
            row = pl.multiple_of(src * depth, depth)
            w_all[pl.ds(row, depth), :] = ws[j * depth : (j + 1) * depth, :]
    for part, xs in enumerate((xa, xb, xa_other, xb_other)):
        both = jnp.dot(
            xs[...], w_all[:, HD:], preferred_element_type=jnp.float32
        ).astype(jnp.bfloat16)
        for i in range(4):
            src = source_of(me, 4 * (part % 2) + i, even, odd, part // 2)
            row = pl.multiple_of(src * rows, rows)
            here = slice(i * rows, (i + 1) * rows)
            keys[pl.ds(row, rows), :] = both[here, :HD]
            values[pl.ds(row, rows), :] = both[here, HD:]
            x_all[pl.ds(pl.multiple_of(row + EDGE, EDGE), rows), :] = xs[here, :]
    wide = rows + 2 * EDGE
    position = lax.broadcasted_iota(jnp.int32, (1, count), 1)
    valid = position < limit
    factor = LOG2E / math.sqrt(HD)
    for mask, out in zip(ALONG_Z, outs):
        start = pl.multiple_of((me ^ mask) * rows, EDGE)
        query = jnp.dot(
            x_all[pl.ds(start, wide), :], w_all[:, :HD], preferred_element_type=jnp.float32
        ).astype(jnp.bfloat16)
        scores = lax.dot_general(
            query, keys[...], (((1,), (1,)), ((), ())), preferred_element_type=jnp.float32
        )
        scores = jnp.where(valid, scores * factor, -1e30)
        weights = jnp.exp2(scores - jnp.max(scores, axis=-1, keepdims=True))
        totals = jnp.sum(weights, axis=-1, keepdims=True)
        summed = jnp.dot(
            weights.astype(jnp.bfloat16), values[...], preferred_element_type=jnp.float32
        )
        out[...] = (summed / totals).astype(jnp.bfloat16)


def bit_of(number, position):
    return (number >> position) & 1


def lane_sources(place, lanes, step):
    block = (lanes % (lanes.shape[1] // 2)) // step
    other = lanes // (lanes.shape[1] // 2)
    origin = place ^ other
    core = origin & 1
    for i, (even, odd) in enumerate(zip(PACK_EVEN, PACK_ODD)):
        origin = origin ^ (bit_of(block, i) * jnp.where(core == 0, even, odd))
    return origin


def tail_kernel(
    scalars, c0, c1, c2, c3, feats, gain, taps, bn_scale, bn_shift, pa, pb, pa_other, pb_other, out,
    wide_gated, *, rows
):
    me, limit = lax.axis_index("frames"), scalars[0]
    place = lax.axis_index("groups") * 16 + me
    held = (pa, pb, pa_other, pb_other)
    wide = rows + 2 * EDGE
    width = out.shape[1]
    quarter = width // 4
    step = pa.shape[0] // 8
    lanes = lax.broadcasted_iota(jnp.int32, (1, width), 1)
    source = lane_sources(place, lanes, step)
    index = (source & 15) * (2 * step) + (source // 16) * step + lanes % step
    line = lax.broadcasted_iota(jnp.int32, (width, width), 0)
    mixing = jnp.where(line == index, 1.0, 0.0).astype(jnp.bfloat16)

    def mixed(array, by):
        return jnp.dot(array, by, preferred_element_type=jnp.float32).astype(jnp.bfloat16)

    def times(array, start, stop):
        total = None
        for i, part in enumerate(held):
            term = jnp.dot(
                array[:, i * quarter : (i + 1) * quarter],
                part[:, start:stop],
                preferred_element_type=jnp.float32,
            )
            total = term if total is None else total + term
        return total

    row_out = (source & 15) * step + lanes % step
    side = source // 16
    heads = [((me ^ mask) // 4) for mask in ALONG_Z]
    spread = 0.0
    small = lax.broadcasted_iota(jnp.int32, (HD, width), 0)
    for head, part in zip(heads, (c0, c1, c2, c3)):
        by = jnp.where(small + head * HD == row_out, 1.0, 0.0).astype(jnp.bfloat16)
        spread = spread + jnp.dot(part[...], by, preferred_element_type=jnp.float32)
    halves = [
        times(
            jnp.where(side == h, spread, 0.0).astype(jnp.bfloat16), 3 * width, 3 * width + width // 2
        )
        for h in range(2)
    ]
    attended = feats[...].astype(jnp.float32) + jnp.concatenate(halves, axis=1)
    mean = jnp.mean(attended, axis=-1, keepdims=True)
    centred = attended - mean
    variance = jnp.mean(centred * centred, axis=-1, keepdims=True)
    normed2 = (centred * lax.rsqrt(variance + EPSILON) * gain[...]).astype(jnp.bfloat16)
    normed2 = mixed(normed2, mixing)
    value = times(normed2, 0, width)
    gate = times(normed2, width, 2 * width)
    frame = me * rows - EDGE + lax.broadcasted_iota(jnp.int32, (wide, 1), 0)
    inside = (frame >= 0) & (frame < limit)
    gated = jnp.where(inside, value * jax.nn.sigmoid(gate), 0.0)
    wide_gated[...] = gated.astype(jnp.bfloat16).astype(jnp.float32)
    half = (taps.shape[0] - 1) // 2
    conv = jnp.zeros((rows, out.shape[1]), jnp.float32)
    for tap in range(taps.shape[0]):
        at = EDGE - half + tap
        conv = conv + taps[tap : tap + 1, :] * wide_gated[at : at + rows, :]
    act = bn_scale[...] * conv + bn_shift[...]
    activated = (act * jax.nn.sigmoid(act)).astype(jnp.bfloat16)
    result = attended[EDGE : EDGE + rows, :] + times(mixed(activated, mixing), 2 * width, 3 * width)
    out[...] = result.astype(jnp.bfloat16)


def per_device(
    features, valid_length, ln1_gain, w_qkv, w_out, ln2_gain, w_pw1, w_dw, bn_scale, bn_shift, w_pw2
):
    rows, width = features.shape
    count = rows * 16
    depth = w_qkv.shape[0]
    groups = lax.axis_size("groups")
    scalars = valid_length
    even, odd = block_masks(ORDER_EVEN), block_masks(ORDER_ODD)
    hbm = pl.BlockSpec(memory_space=pltpu.HBM)
    smem = pl.BlockSpec(memory_space=pltpu.SMEM)
    vmem = pl.BlockSpec(memory_space=pltpu.VMEM)

    normed1, w_mine, w_12, w_4, w_8, pack = pl.pallas_call(
        prepare_kernel,
        name="prepare",
        out_shape=[jax.ShapeDtypeStruct((rows, width), jnp.bfloat16)]
        + [jax.ShapeDtypeStruct((depth, 3 * HD), jnp.bfloat16)] * 4
        + [jax.ShapeDtypeStruct((depth // 2, 3 * width + width // 2), jnp.bfloat16)],
        in_specs=[smem, hbm, vmem] + [hbm] * 4,
        out_specs=[vmem] * 6,
        scratch_shapes=[
            pltpu.VMEM((rows, width), jnp.bfloat16),
            pltpu.SemaphoreType.DMA((16,)),
        ],
        compiler_params=pltpu.CompilerParams(vmem_limit_bytes=60 << 20),
    )(scalars, features, ln1_gain.reshape(1, -1), w_qkv, w_out, w_pw1, w_pw2)

    def joined(*arrays):
        return lax.optimization_barrier(jnp.concatenate(arrays, axis=0))

    def pack_swap(held, stage):
        return swap(held, PACK_EVEN[stage], PACK_ODD[stage], groups)

    ahead = lax.ppermute(features[-EDGE:], "frames", [(i, i + 1) for i in range(15)])
    behind = lax.ppermute(features[:EDGE], "frames", [(i + 1, i) for i in range(15)])
    x1 = swap(normed1, ORDER_EVEN[0], ORDER_ODD[0])
    w_z = [swap(part, mask) for part, mask in zip((w_12, w_4, w_8), ALONG_Z[1:])]
    p2 = joined(pack, pack_swap(pack, 0))
    x2 = joined(normed1, x1)
    w4 = joined(w_mine, *w_z)
    w8 = joined(w4, swap(w4, 2))
    p2, w8, x2, ahead, behind = lax.optimization_barrier((p2, w8, x2, ahead, behind))

    p4 = joined(p2, pack_swap(p2, 1))
    xa = joined(x2, swap(x2, ORDER_EVEN[1], ORDER_ODD[1]))
    w_other = swap(w8, 1)
    xa, w_other = lax.optimization_barrier((xa, w_other))

    xb = swap(xa, ORDER_EVEN[2], ORDER_ODD[2])
    xa_other = swap(xa, 1)
    pa = joined(p4, pack_swap(p4, 2))
    xb_other = swap(xb, 1)
    pb = pack_swap(pa, 3)
    pa_other = swap(pa, 1)

    wide = rows + 2 * EDGE
    w_masks = list(ALONG_Z) + [mask ^ 2 for mask in ALONG_Z]
    contexts = pl.pallas_call(
        functools.partial(
            attention_kernel, rows=rows, even=even, odd=odd, w_masks=w_masks, count=count
        ),
        name="attention",
        out_shape=[jax.ShapeDtypeStruct((wide, HD), jnp.bfloat16)] * 4,
        in_specs=[smem] + [vmem] * 6,
        out_specs=[vmem] * 4,
        scratch_shapes=[
            pltpu.VMEM((count + 2 * EDGE, width), jnp.bfloat16),
            pltpu.VMEM((16 * depth, 3 * HD), jnp.bfloat16),
            pltpu.VMEM((count, HD), jnp.bfloat16),
            pltpu.VMEM((count, HD), jnp.bfloat16),
        ],
        compiler_params=pltpu.CompilerParams(vmem_limit_bytes=40 << 20),
        cost_estimate=pl.CostEstimate(
            flops=6_000_000_000, bytes_accessed=8 << 20, transcendentals=4 * wide * count
        ),
    )(scalars, xa, xb, xa_other, xb_other, w8, w_other)
    mine = [contexts[0]] + [swap(part, mask) for part, mask in zip(contexts[1:], ALONG_Z[1:])]
    pb, _ = lax.optimization_barrier((pb, mine))
    pb_other = swap(pb, 1)

    feats = jnp.concatenate([ahead, features, behind], axis=0)
    return pl.pallas_call(
        functools.partial(tail_kernel, rows=rows),
        name="tail",
        out_shape=jax.ShapeDtypeStruct((rows, width), jnp.bfloat16),
        in_specs=[smem] + [vmem] * 13,
        out_specs=vmem,
        scratch_shapes=[
            pltpu.VMEM((wide, width), jnp.float32),
        ],
        compiler_params=pltpu.CompilerParams(vmem_limit_bytes=40 << 20),
        cost_estimate=pl.CostEstimate(
            flops=1_200_000_000, bytes_accessed=8 << 20, transcendentals=wide * width * 2
        ),
    )(
        scalars,
        *mine,
        feats,
        ln2_gain.reshape(1, -1),
        w_dw,
        bn_scale.reshape(1, -1),
        bn_shift.reshape(1, -1),
        pa,
        pb,
        pa_other,
        pb_other,
    )


def solution(mesh):
    placed = (
        P(("groups", "frames"), None),
        P("groups"),
        P(),
        P("frames", None),
        P("frames", None),
        P(),
        P("frames", None),
        P(),
        P(),
        P(),
        P("frames", None),
    )
    return jax.shard_map(
        per_device if (mesh.shape["groups"], mesh.shape["frames"]) == (2, 16) else per_device_general,
        mesh=mesh,
        in_specs=placed,
        out_specs=P(("groups", "frames"), None),
        check_vma=False,
    )
```

```python
import functools
import math

import jax
import jax.numpy as jnp
from jax import lax
from jax.experimental import pallas as pl
from jax.experimental.pallas import tpu as pltpu
from jax.sharding import PartitionSpec as P

HEADS = 4
HD = 128

EPSILON = 1e-05
EDGE = 16
LOG2E = 1.4426950408889634

ORDER_EVEN = (8, 4, 2)
ORDER_ODD = (2, 8, 4)
PACK_EVEN = (8, 2, 16, 4)
PACK_ODD = (8, 4, 16, 2)
ALONG_Z = (0, 12, 4, 8)


def extended(cells, sides, width):
    for axis, dim in sides:
        count = lax.axis_size(axis)
        ends = count - 1
        head = lax.slice_in_dim(cells, 0, width, axis=dim)
        tail = lax.slice_in_dim(cells, cells.shape[dim] - width, cells.shape[dim], axis=dim)
        cells = jnp.concatenate(
            [
                lax.ppermute(tail, axis, [(i, (i + 1) % count) for i in range(ends)]),
                cells,
                lax.ppermute(head, axis, [((i + 1) % count, i) for i in range(ends)]),
            ],
            axis=dim,
        )
    return cells


def layer_norm(values, gain):
    values = values.astype(jnp.float32)
    mean = jnp.mean(values, axis=-1, keepdims=True)
    centred = values - mean
    variance = jnp.mean(centred * centred, axis=-1, keepdims=True)
    return (centred * lax.rsqrt(variance + EPSILON) * gain).astype(jnp.bfloat16)


def per_device_general(
    features, valid_length, ln1_gain, w_qkv, w_out, ln2_gain, w_pw1, w_dw, bn_scale, bn_shift, w_pw2
):
    limit = valid_length[0]
    local_rows = features.shape[0]
    width = features.shape[1]
    att_width = w_qkv.shape[1] // 3
    scale = 1.0 / math.sqrt(HD)
    full_out = lax.all_gather(w_out, "frames", axis=0, tiled=True)
    full_pw1 = lax.all_gather(w_pw1, "frames", axis=0, tiled=True)
    full_pw2 = lax.all_gather(w_pw2, "frames", axis=0, tiled=True)
    normed1 = layer_norm(features, ln1_gain)
    qkv = jnp.dot(
        normed1,
        lax.all_gather(w_qkv, "frames", axis=0, tiled=True),
        preferred_element_type=jnp.float32,
    ).astype(jnp.bfloat16)
    query_heads = qkv[:, :att_width].reshape(local_rows, HEADS, HD)
    pairs = lax.all_gather(qkv[:, att_width:], "frames", axis=0, tiled=True)
    count = pairs.shape[0]
    key_heads = pairs[:, :att_width].reshape(count, HEADS, HD)
    value_heads = pairs[:, att_width:].reshape(count, HEADS, HD)
    scores = (
        jnp.einsum("qhd,khd->hqk", query_heads, key_heads, preferred_element_type=jnp.float32)
        * scale
    )
    valid = (jnp.arange(count, dtype=jnp.int32) < limit)[None, None, :]
    scores = jnp.where(valid, scores, -1e30)
    maxima = jnp.max(scores, axis=-1)
    weights = jnp.where(valid, jnp.exp(scores - maxima[..., None]), 0.0)
    totals = jnp.sum(weights, axis=-1)
    summed = jnp.einsum(
        "hqk,khd->hqd",
        weights.astype(jnp.bfloat16),
        value_heads,
        preferred_element_type=jnp.float32,
    )
    context = (
        (summed / totals[..., None])
        .transpose(1, 0, 2)
        .reshape(local_rows, att_width)
        .astype(jnp.bfloat16)
    )
    attended = features.astype(jnp.float32) + jnp.dot(
        context, full_out, preferred_element_type=jnp.float32
    )
    normed2 = layer_norm(attended, ln2_gain)
    both = jnp.dot(normed2, full_pw1, preferred_element_type=jnp.float32)
    frame_index = lax.axis_index("frames") * local_rows + jnp.arange(local_rows, dtype=jnp.int32)
    frame_valid = (frame_index < limit)[:, None]
    gated = jnp.where(frame_valid, both[:, :width] * jax.nn.sigmoid(both[:, width:]), 0.0).astype(
        jnp.bfloat16
    )
    half_window = (w_dw.shape[0] - 1) // 2
    widened = extended(gated, (("frames", 0),), half_window).astype(jnp.float32)
    conv = jnp.zeros((local_rows, width), jnp.float32)
    for tap in range(w_dw.shape[0]):
        conv = conv + w_dw[tap][None, :] * widened[tap : tap + local_rows]
    activated = jax.nn.silu(bn_scale * conv + bn_shift).astype(jnp.bfloat16)
    result = attended + jnp.dot(activated, full_pw2, preferred_element_type=jnp.float32)
    return result.astype(jnp.bfloat16)


def swap(array, even, odd=None, groups=None):
    odd = even if odd is None else odd
    if groups is None:
        pairs = [(i, i ^ (odd if i & 1 else even)) for i in range(16)]
        return lax.ppermute(array, "frames", pairs)
    pairs = [(i, i ^ (odd if i & 1 else even)) for i in range(16 * groups)]
    return lax.ppermute(array, ("groups", "frames"), pairs)


def block_masks(order):
    masks = [0]
    for bit in order:
        masks = masks + [mask ^ bit for mask in masks]
    return masks


def source_of(me, j, even, odd, other_core):
    origin = me ^ 1 if other_core else me
    core = origin & 1
    return origin ^ jnp.where(core == 0, even[j], odd[j])


def prepare_kernel(
    scalars, feats_in, gain, w_qkv, w_out, w_pw1, w_pw2, normed, head0, head1, head2, head3, pack, feats, sems
):
    me, group = lax.axis_index("frames"), lax.axis_index("groups")
    load = pltpu.make_async_copy(feats_in, feats, sems.at[0])
    load.start()
    att = w_qkv.shape[1] // 3
    width = feats.shape[1]
    copies = []
    for mask, out in zip(ALONG_Z, (head0, head1, head2, head3)):
        head = (me ^ mask) // 4
        for i in range(3):
            start = pl.multiple_of(i * att + head * HD, HD)
            copies.append((w_qkv.at[:, pl.ds(start, HD)], out.at[:, i * HD : (i + 1) * HD]))
    half = pack.shape[0]
    start = pl.multiple_of(group * half, half)
    copies.append((w_pw1.at[pl.ds(start, half)], pack.at[:, 0 : 2 * width]))
    copies.append((w_pw2.at[pl.ds(start, half)], pack.at[:, 2 * width : 3 * width]))
    side = pl.multiple_of(group * (width // 2), width // 2)
    copies.append((w_out.at[:, pl.ds(side, width // 2)], pack.at[:, 3 * width :]))
    copies = [pltpu.make_async_copy(a, b, sems.at[1 + i]) for i, (a, b) in enumerate(copies)]
    for copy in copies:
        copy.start()
    load.wait()
    values = feats[...].astype(jnp.float32)
    mean = jnp.mean(values, axis=-1, keepdims=True)
    centred = values - mean
    variance = jnp.mean(centred * centred, axis=-1, keepdims=True)
    normed[...] = (centred * lax.rsqrt(variance + EPSILON) * gain[...]).astype(jnp.bfloat16)
    for copy in copies:
        copy.wait()


def attention_kernel(
    scalars, xa, xb, xa_other, xb_other, own_w, other_w, *refs, rows, even, odd, w_masks, count
):
    outs, (x_all, w_all, keys, values) = refs[:4], refs[4:]
    me, limit = lax.axis_index("frames"), scalars[0]
    depth = w_all.shape[0] // 16
    width = x_all.shape[1]
    x_all[0:EDGE, :] = jnp.zeros((EDGE, width), jnp.bfloat16)
    x_all[EDGE + count : 2 * EDGE + count, :] = jnp.zeros((EDGE, width), jnp.bfloat16)
    for other_core, ws in enumerate((own_w, other_w)):
        for j in range(8):
            src = source_of(me, j, w_masks, w_masks, other_core)
            row = pl.multiple_of(src * depth, depth)
            w_all[pl.ds(row, depth), :] = ws[j * depth : (j + 1) * depth, :]
    for part, xs in enumerate((xa, xb, xa_other, xb_other)):
        both = jnp.dot(
            xs[...], w_all[:, HD:], preferred_element_type=jnp.float32
        ).astype(jnp.bfloat16)
        for i in range(4):
            src = source_of(me, 4 * (part % 2) + i, even, odd, part // 2)
            row = pl.multiple_of(src * rows, rows)
            here = slice(i * rows, (i + 1) * rows)
            keys[pl.ds(row, rows), :] = both[here, :HD]
            values[pl.ds(row, rows), :] = both[here, HD:]
            x_all[pl.ds(pl.multiple_of(row + EDGE, EDGE), rows), :] = xs[here, :]
    wide = rows + 2 * EDGE
    position = lax.broadcasted_iota(jnp.int32, (1, count), 1)
    valid = position < limit
    factor = LOG2E / math.sqrt(HD)
    for mask, out in zip(ALONG_Z, outs):
        start = pl.multiple_of((me ^ mask) * rows, EDGE)
        query = jnp.dot(
            x_all[pl.ds(start, wide), :], w_all[:, :HD], preferred_element_type=jnp.float32
        ).astype(jnp.bfloat16)
        scores = lax.dot_general(
            query, keys[...], (((1,), (1,)), ((), ())), preferred_element_type=jnp.float32
        )
        scores = jnp.where(valid, scores * factor, -1e30)
        weights = jnp.exp2(scores - jnp.max(scores, axis=-1, keepdims=True))
        totals = jnp.sum(weights, axis=-1, keepdims=True)
        summed = jnp.dot(
            weights.astype(jnp.bfloat16), values[...], preferred_element_type=jnp.float32
        )
        out[...] = (summed / totals).astype(jnp.bfloat16)


def bit_of(number, position):
    return (number >> position) & 1


def lane_sources(place, lanes, step):
    block = (lanes % (lanes.shape[1] // 2)) // step
    other = lanes // (lanes.shape[1] // 2)
    origin = place ^ other
    core = origin & 1
    for i, (even, odd) in enumerate(zip(PACK_EVEN, PACK_ODD)):
        origin = origin ^ (bit_of(block, i) * jnp.where(core == 0, even, odd))
    return origin


def tail_kernel(
    scalars, c0, c1, c2, c3, feats, gain, taps, bn_scale, bn_shift, pa, pb, pa_other, pb_other, out,
    wide_gated, *, rows
):
    me, limit = lax.axis_index("frames"), scalars[0]
    place = lax.axis_index("groups") * 16 + me
    held = (pa, pb, pa_other, pb_other)
    wide = rows + 2 * EDGE
    width = out.shape[1]
    quarter = width // 4
    step = pa.shape[0] // 8
    lanes = lax.broadcasted_iota(jnp.int32, (1, width), 1)
    source = lane_sources(place, lanes, step)
    index = (source & 15) * (2 * step) + (source // 16) * step + lanes % step
    line = lax.broadcasted_iota(jnp.int32, (width, width), 0)
    mixing = jnp.where(line == index, 1.0, 0.0).astype(jnp.bfloat16)

    def mixed(array, by):
        return jnp.dot(array, by, preferred_element_type=jnp.float32).astype(jnp.bfloat16)

    def times(array, start, stop):
        total = None
        for i, part in enumerate(held):
            term = jnp.dot(
                array[:, i * quarter : (i + 1) * quarter],
                part[:, start:stop],
                preferred_element_type=jnp.float32,
            )
            total = term if total is None else total + term
        return total

    row_out = (source & 15) * step + lanes % step
    side = source // 16
    heads = [((me ^ mask) // 4) for mask in ALONG_Z]
    spread = 0.0
    small = lax.broadcasted_iota(jnp.int32, (HD, width), 0)
    for head, part in zip(heads, (c0, c1, c2, c3)):
        by = jnp.where(small + head * HD == row_out, 1.0, 0.0).astype(jnp.bfloat16)
        spread = spread + jnp.dot(part[...], by, preferred_element_type=jnp.float32)
    halves = [
        times(
            jnp.where(side == h, spread, 0.0).astype(jnp.bfloat16), 3 * width, 3 * width + width // 2
        )
        for h in range(2)
    ]
    attended = feats[...].astype(jnp.float32) + jnp.concatenate(halves, axis=1)
    mean = jnp.mean(attended, axis=-1, keepdims=True)
    centred = attended - mean
    variance = jnp.mean(centred * centred, axis=-1, keepdims=True)
    normed2 = (centred * lax.rsqrt(variance + EPSILON) * gain[...]).astype(jnp.bfloat16)
    normed2 = mixed(normed2, mixing)
    value = times(normed2, 0, width)
    gate = times(normed2, width, 2 * width)
    frame = me * rows - EDGE + lax.broadcasted_iota(jnp.int32, (wide, 1), 0)
    inside = (frame >= 0) & (frame < limit)
    gated = jnp.where(inside, value * jax.nn.sigmoid(gate), 0.0)
    wide_gated[...] = gated.astype(jnp.bfloat16).astype(jnp.float32)
    half = (taps.shape[0] - 1) // 2
    conv = jnp.zeros((rows, out.shape[1]), jnp.float32)
    for tap in range(taps.shape[0]):
        at = EDGE - half + tap
        conv = conv + taps[tap : tap + 1, :] * wide_gated[at : at + rows, :]
    act = bn_scale[...] * conv + bn_shift[...]
    activated = (act * jax.nn.sigmoid(act)).astype(jnp.bfloat16)
    result = attended[EDGE : EDGE + rows, :] + times(mixed(activated, mixing), 2 * width, 3 * width)
    out[...] = result.astype(jnp.bfloat16)


def per_device(
    features, valid_length, ln1_gain, w_qkv, w_out, ln2_gain, w_pw1, w_dw, bn_scale, bn_shift, w_pw2
):
    rows, width = features.shape
    count = rows * 16
    depth = w_qkv.shape[0]
    groups = lax.axis_size("groups")
    scalars = valid_length
    even, odd = block_masks(ORDER_EVEN), block_masks(ORDER_ODD)
    hbm = pl.BlockSpec(memory_space=pltpu.HBM)
    smem = pl.BlockSpec(memory_space=pltpu.SMEM)
    vmem = pl.BlockSpec(memory_space=pltpu.VMEM)

    normed1, w_mine, w_12, w_4, w_8, pack = pl.pallas_call(
        prepare_kernel,
        name="prepare",
        out_shape=[jax.ShapeDtypeStruct((rows, width), jnp.bfloat16)]
        + [jax.ShapeDtypeStruct((depth, 3 * HD), jnp.bfloat16)] * 4
        + [jax.ShapeDtypeStruct((depth // 2, 3 * width + width // 2), jnp.bfloat16)],
        in_specs=[smem, hbm, vmem] + [hbm] * 4,
        out_specs=[vmem] * 6,
        scratch_shapes=[
            pltpu.VMEM((rows, width), jnp.bfloat16),
            pltpu.SemaphoreType.DMA((16,)),
        ],
        compiler_params=pltpu.CompilerParams(vmem_limit_bytes=60 << 20),
    )(scalars, features, ln1_gain.reshape(1, -1), w_qkv, w_out, w_pw1, w_pw2)

    def joined(*arrays):
        return lax.optimization_barrier(jnp.concatenate(arrays, axis=0))

    def pack_swap(held, stage):
        return swap(held, PACK_EVEN[stage], PACK_ODD[stage], groups)

    ahead = lax.ppermute(features[-EDGE:], "frames", [(i, i + 1) for i in range(15)])
    behind = lax.ppermute(features[:EDGE], "frames", [(i + 1, i) for i in range(15)])
    x1 = swap(normed1, ORDER_EVEN[0], ORDER_ODD[0])
    w_z = [swap(part, mask) for part, mask in zip((w_12, w_4, w_8), ALONG_Z[1:])]
    p2 = joined(pack, pack_swap(pack, 0))
    x2 = joined(normed1, x1)
    w4 = joined(w_mine, *w_z)
    w8 = joined(w4, swap(w4, 2))
    p2, w8, x2, ahead, behind = lax.optimization_barrier((p2, w8, x2, ahead, behind))

    p4 = joined(p2, pack_swap(p2, 1))
    xa = joined(x2, swap(x2, ORDER_EVEN[1], ORDER_ODD[1]))
    w_other = swap(w8, 1)
    xa, w_other = lax.optimization_barrier((xa, w_other))

    xb = swap(xa, ORDER_EVEN[2], ORDER_ODD[2])
    xa_other = swap(xa, 1)
    pa = joined(p4, pack_swap(p4, 2))
    xb_other = swap(xb, 1)
    pb = pack_swap(pa, 3)
    pa_other = swap(pa, 1)

    wide = rows + 2 * EDGE
    w_masks = list(ALONG_Z) + [mask ^ 2 for mask in ALONG_Z]
    contexts = pl.pallas_call(
        functools.partial(
            attention_kernel, rows=rows, even=even, odd=odd, w_masks=w_masks, count=count
        ),
        name="attention",
        out_shape=[jax.ShapeDtypeStruct((wide, HD), jnp.bfloat16)] * 4,
        in_specs=[smem] + [vmem] * 6,
        out_specs=[vmem] * 4,
        scratch_shapes=[
            pltpu.VMEM((count + 2 * EDGE, width), jnp.bfloat16),
            pltpu.VMEM((16 * depth, 3 * HD), jnp.bfloat16),
            pltpu.VMEM((count, HD), jnp.bfloat16),
            pltpu.VMEM((count, HD), jnp.bfloat16),
        ],
        compiler_params=pltpu.CompilerParams(vmem_limit_bytes=40 << 20),
        cost_estimate=pl.CostEstimate(
            flops=5_000_000_000, bytes_accessed=8 << 20, transcendentals=4 * wide * count
        ),
    )(scalars, xa, xb, xa_other, xb_other, w8, w_other)
    mine = [contexts[0]] + [swap(part, mask) for part, mask in zip(contexts[1:], ALONG_Z[1:])]
    pb, _ = lax.optimization_barrier((pb, mine))
    pb_other = swap(pb, 1)

    feats = jnp.concatenate([ahead, features, behind], axis=0)
    return pl.pallas_call(
        functools.partial(tail_kernel, rows=rows),
        name="tail",
        out_shape=jax.ShapeDtypeStruct((rows, width), jnp.bfloat16),
        in_specs=[smem] + [vmem] * 13,
        out_specs=vmem,
        scratch_shapes=[
            pltpu.VMEM((wide, width), jnp.float32),
        ],
        compiler_params=pltpu.CompilerParams(vmem_limit_bytes=40 << 20),
        cost_estimate=pl.CostEstimate(
            flops=1_200_000_000, bytes_accessed=8 << 20, transcendentals=wide * width * 2
        ),
    )(
        scalars,
        *mine,
        feats,
        ln2_gain.reshape(1, -1),
        w_dw,
        bn_scale.reshape(1, -1),
        bn_shift.reshape(1, -1),
        pa,
        pb,
        pa_other,
        pb_other,
    )


def solution(mesh):
    placed = (
        P(("groups", "frames"), None),
        P("groups"),
        P(),
        P("frames", None),
        P("frames", None),
        P(),
        P("frames", None),
        P(),
        P(),
        P(),
        P("frames", None),
    )
    return jax.shard_map(
        per_device if (mesh.shape["groups"], mesh.shape["frames"]) == (2, 16) else per_device_general,
        mesh=mesh,
        in_specs=placed,
        out_specs=P(("groups", "frames"), None),
        check_vma=False,
    )
```
